32 devices in a mesh: ctx: 8 (over y, x, core), exp: 4 (over z).
Axes of the slice: x: 2, y: 2, z: 4, core: 2. Of those that a mesh axis runs over, the one named last changes fastest.
Arguments:
- queries: bfloat16 [4096, 4096], P(('ctx', 'exp')), may hold values from -100 to 100
- keys: bfloat16 [4096, 1024], P(('ctx', 'exp')), may hold values from -100 to 100
- values: bfloat16 [4096, 1024], P(('ctx', 'exp')), may hold values from -6 to 6
- doc_ids: int32 [4096], P(('ctx', 'exp')), may hold values from 0 to 7, never falling along the last dimension, each value on 1 to 1024 neighbouring positions
- span_ids: int32 [4096], P(('ctx', 'exp')), may hold values from 0 to 3, never falling along the last dimension, each value on 1 to 2048 neighbouring positions
Outputs:
- attended: bfloat16 [4096, 4096], P(('ctx', 'exp'))
The draws below stay inside these ranges and needn't reach their ends.
Inputs may be any that keep to these rules, and one draw needn't show every extreme that they name: `doc_ids`: never falling; each document has 1 to 1024 positions, one exactly 1024. `span_ids`: never falling; each span has 1 to 2048 positions, one exactly 2048.
All inputs are finite; a program needn't handle non-finite values.
Results may differ from the reference program's by a relative error of at most 0.0061.
Values may be sent and summed in bfloat16 or wider, within the bound.
A program may use at most 64 MiB of HBM per device.

```python
import math
import jax
import jax.numpy as jnp
import numpy as np
from jax import lax

QUERY_HEADS = 32
KEY_VALUE_HEADS = 8
HEAD_SIZE = 128
SPAN = 8192
DOC_LEN = 2048
PACKED_TOKENS = 4096
SPAN_TOP = 2048
DOC_TOP = 1024
SPANS = 4
DOCS = 8


def broadcast_heads(key, heads):
    key_base, key_rows, key_cols = jax.random.split(key, 3)
    normal_part = jax.random.truncated_normal(key_base, -4.0, 4.0, (PACKED_TOKENS, heads, HEAD_SIZE), jnp.float32)
    row_scale = jnp.exp(jax.random.uniform(key_rows, (PACKED_TOKENS, heads, 1), jnp.float32, 0.0, math.log(10.0)))
    column_scale = jax.random.uniform(key_cols, (1, heads, HEAD_SIZE), jnp.float32, 0.5, 1.5)
    return (normal_part * row_scale * column_scale).reshape(PACKED_TOKENS, heads * HEAD_SIZE)


def draw_queries(key, part):
    return broadcast_heads(jax.random.fold_in(key, 11), QUERY_HEADS).astype(jnp.bfloat16)


def draw_keys(key, part):
    return broadcast_heads(jax.random.fold_in(key, 23), KEY_VALUE_HEADS).astype(jnp.bfloat16)


def steps_of(key, dims, shards, smallest, top_value):
    def one(dim, blocks):
        draws = jax.random.uniform(jax.random.fold_in(jax.random.fold_in(key, 6), dim), (blocks,), jnp.float32, smallest / len(shards), top_value / len(shards))
        return jnp.repeat(jnp.exp(draws), dims[dim] // blocks).reshape((-1,) + (1,) * (len(dims) - dim - 1))

    factor_of = one(*shards[0])
    for cut in shards[1:]:
        factor_of = factor_of * one(*cut)
    return factor_of


def length_profile(number_of, total, reach, skew):
    weights = [(1 << 20) // math.isqrt(grade ** skew) + 1 for grade in range(2, number_of + 1)]
    rest, given = total - reach - (number_of - 1), [1] * (number_of - 1)
    while rest > 0:
        movable = [i for i in range(number_of - 1) if given[i] < reach]
        mass, remaining = sum([weights[i] for i in movable]), rest
        for i in movable:
            more = min(reach - given[i], max(1, remaining * weights[i] // mass), rest)
            given[i] = given[i] + more
            rest = rest - more
    return np.array([reach] + given)


def ragged(own_key, amount, total, limit, lean):
    if amount == 2:
        one = jax.random.randint(own_key, (), max(1, total - limit), min(limit, total - 1) + 1)
        return jnp.stack([one, total - one])
    sizes = jnp.asarray(length_profile(amount, total, limit, lean), jnp.int32)
    twos = (amount - 1) // 2
    donor, sink = sizes[1:1 + 2 * twos:2], sizes[2:2 + 2 * twos:2]
    slack = jnp.minimum(donor - 1, limit - sink)
    moved = jax.random.randint(jax.random.fold_in(own_key, 1), (twos,), 0, 1 << 20) % (slack + 1)
    sizes = sizes.at[1:1 + 2 * twos:2].set(donor - moved).at[2:2 + 2 * twos:2].set(sink + moved)
    return sizes[jax.random.permutation(jax.random.fold_in(own_key, 2), amount)]


def bell_draw(stream_key, shape, spread, limit, shards=(), kind=jnp.bfloat16):
    loudness = steps_of(stream_key, shape, shards, -0.22, 0.18) if shards else 1.0
    drawn = jax.random.normal(stream_key, shape, jnp.float32) * spread * loudness
    return jnp.minimum(jnp.maximum(drawn, -limit), limit).astype(kind)


def setup_inputs(seed: int = 0) -> dict:
    arg_keys = jax.random.split(jax.random.key(seed), 6)
    queries = draw_queries(jax.random.fold_in(arg_keys[5], 71), 0)
    keys = draw_keys(jax.random.fold_in(arg_keys[5], 71), 0)
    values = bell_draw(arg_keys[2], (PACKED_TOKENS, KEY_VALUE_HEADS * HEAD_SIZE), 1.0, 6.0, ((0, 32),))
    doc_ids = jnp.searchsorted(jnp.cumsum(ragged(arg_keys[3], DOCS, PACKED_TOKENS, DOC_TOP, 1)), jnp.arange(PACKED_TOKENS), side="right").astype(jnp.int32)
    span_ids = jnp.searchsorted(jnp.cumsum(ragged(arg_keys[4], SPANS, PACKED_TOKENS, SPAN_TOP, 1)), jnp.arange(PACKED_TOKENS), side="right").astype(jnp.int32)
    return {"queries": queries, "keys": keys, "values": values, "doc_ids": doc_ids, "span_ids": span_ids}


def single_unit_rows(tensor):
    widened = tensor.astype(jnp.float32)
    factor = lax.rsqrt(lax.optimization_barrier(jnp.mean(widened * widened, axis=-1, keepdims=True)) + 1e-06)
    return (widened * factor).astype(jnp.bfloat16)

def reference(queries, keys, values, doc_ids, span_ids):
    overall_rows = queries.shape[0]
    query_heads = single_unit_rows(queries.reshape(overall_rows, QUERY_HEADS, HEAD_SIZE))
    key_head_rows = single_unit_rows(keys.reshape(overall_rows, KEY_VALUE_HEADS, HEAD_SIZE))
    value_head_rows = values.reshape(overall_rows, KEY_VALUE_HEADS, HEAD_SIZE)
    query_group_width = QUERY_HEADS // KEY_VALUE_HEADS
    tile_length = min(512, overall_rows)
    reach_len = min(SPAN, DOC_LEN)
    lookback = (reach_len - 1 + tile_length - 1) // tile_length * tile_length
    window = min(overall_rows, lookback + tile_length)
    offsets_q = jnp.arange(tile_length, dtype=jnp.int32)
    offsets_k = jnp.arange(window, dtype=jnp.int32)

    def one_block(block_num):
        q_first = (block_num * tile_length).astype(jnp.int32)
        k_first = jnp.clip(q_first - lookback, 0, overall_rows - window).astype(jnp.int32)
        query_tile = lax.dynamic_slice_in_dim(query_heads, q_first, tile_length).astype(jnp.float32)
        query_tile = query_tile.reshape(tile_length, KEY_VALUE_HEADS, query_group_width, HEAD_SIZE)
        k_tile = lax.dynamic_slice_in_dim(key_head_rows, k_first, window).astype(jnp.float32)
        v_tile = lax.dynamic_slice_in_dim(value_head_rows, k_first, window).astype(jnp.float32)
        scores = jnp.einsum('qhgd,khd->qhgk', query_tile, k_tile) * HEAD_SIZE ** (-0.5)
        q_pos = q_first + offsets_q
        k_pos = k_first + offsets_k
        q_doc = lax.dynamic_slice_in_dim(doc_ids, q_first, tile_length)
        k_doc = lax.dynamic_slice_in_dim(doc_ids, k_first, window)
        q_span = lax.dynamic_slice_in_dim(span_ids, q_first, tile_length)
        k_span = lax.dynamic_slice_in_dim(span_ids, k_first, window)
        allowed = (q_doc[:, None] == k_doc[None, :]) & (q_span[:, None] == k_span[None, :]) & (k_pos[None, :] <= q_pos[:, None])
        weights = jnp.where(allowed[:, None, None, :], jnp.exp(scores), 0.0)
        totals = lax.optimization_barrier(jnp.sum(weights, axis=3))
        rounded = lax.optimization_barrier(weights.astype(jnp.bfloat16)).astype(jnp.float32)
        numerator = jnp.einsum('qhgk,khd->qhgd', rounded, v_tile)
        return (numerator / totals[..., None]).astype(jnp.bfloat16).reshape(tile_length, QUERY_HEADS * HEAD_SIZE)
    blocks = lax.map(one_block, jnp.arange(overall_rows // tile_length, dtype=jnp.int32))
    return blocks.reshape(overall_rows, QUERY_HEADS * HEAD_SIZE)
```

```python
import math

import jax
import jax.numpy as jnp
from jax import lax
from jax.experimental import pallas as pl
from jax.experimental.pallas import tpu as pltpu
from jax.sharding import PartitionSpec as P

QUERY_HEADS = 32
KEY_VALUE_HEADS = 8
HEAD_SIZE = 128
SPAN = 8192
DOC_LEN = 2048
PACKED_TOKENS = 4096
DOC_TOP = 1024
GROUP = QUERY_HEADS // KEY_VALUE_HEADS
MESH = pl.DeviceIdType.MESH


def shifted(block, axis, distance):
    devices = range(lax.axis_size(axis))
    route = [(i - distance, i) for i in devices if i - distance in devices]
    return lax.ppermute(block, axis, route)


def single_unit_rows(tensor):
    widened = tensor.astype(jnp.float32)
    factor = lax.rsqrt(jnp.mean(widened * widened, axis=-1, keepdims=True) + 1e-06)
    return (widened * factor).astype(jnp.bfloat16)


def general(queries, keys, values, doc_ids, span_ids):
    expanded_size = lax.axis_size("exp")
    ctx_size = lax.axis_size("ctx")
    shard_rows = queries.shape[0]
    shard_len = shard_rows * expanded_size
    query_heads = single_unit_rows(queries.reshape(shard_rows, QUERY_HEADS, HEAD_SIZE))
    key_head_rows = single_unit_rows(keys.reshape(shard_rows, KEY_VALUE_HEADS, HEAD_SIZE))
    value_head_rows = values.reshape(shard_rows, KEY_VALUE_HEADS, HEAD_SIZE)
    head_replicas = max(1, expanded_size // KEY_VALUE_HEADS)
    reach_len = min(SPAN, DOC_LEN)
    steps_back = min((reach_len - 2) // shard_len + 1, ctx_size - 1)
    raw_pair = jnp.concatenate([key_head_rows, value_head_rows], axis=2)

    def spread(pair_rows):
        if head_replicas > 1:
            return jnp.repeat(pair_rows, head_replicas, axis=1)
        return pair_rows

    sources = []
    paired = spread(raw_pair)
    query_local, pair_local = (
        lax.all_to_all(query_heads, "exp", split_axis=1, concat_axis=0, tiled=True),
        lax.all_to_all(paired, "exp", split_axis=1, concat_axis=0, tiled=True),
    )
    block_doc, block_span = (
        lax.all_gather(doc_ids, "exp", axis=0, tiled=True),
        lax.all_gather(span_ids, "exp", axis=0, tiled=True),
    )
    sources.append((0, pair_local, block_doc, block_span))
    for distance in range(1, steps_back + 1):
        moved = shifted(pair_local, "ctx", distance)
        moved_doc, moved_span = shifted((block_doc, block_span), "ctx", distance)
        sources.append((distance, moved, moved_doc, moved_span))
    block_doc = sources[0][2]
    block_span = sources[0][3]
    local_heads = query_local.shape[1]
    pair_heads = sources[0][1].shape[1]
    query_group_width = local_heads // pair_heads
    ctx_index = lax.axis_index("ctx")
    tile_length = min(512, shard_len)
    tiles_side = shard_len // tile_length
    query_start = ctx_index * shard_len
    grouped = query_local.reshape(shard_len, pair_heads, query_group_width, HEAD_SIZE)
    inv_root = HEAD_SIZE ** (-0.5)
    offsets = jnp.arange(tile_length, dtype=jnp.int32)
    query_doc_tiles = block_doc.reshape(tiles_side, tile_length)
    query_span_tiles = block_span.reshape(tiles_side, tile_length)
    numer_list = [
        jnp.zeros((tile_length, pair_heads, query_group_width, HEAD_SIZE), jnp.float32)
        for _ in range(tiles_side)
    ]
    denom_list = [
        jnp.zeros((tile_length, pair_heads, query_group_width), jnp.float32)
        for _ in range(tiles_side)
    ]
    for distance, source, key_doc, key_span in sources:
        key_start = query_start - distance * shard_len
        present = ctx_index >= distance
        key_doc_tiles = key_doc.reshape(tiles_side, tile_length)
        key_span_tiles = key_span.reshape(tiles_side, tile_length)
        live_table = (
            (key_doc_tiles[None, :, tile_length - 1] >= query_doc_tiles[:, None, 0])
            & (key_span_tiles[None, :, tile_length - 1] >= query_span_tiles[:, None, 0])
            & present
        )
        for q_block in range(tiles_side):
            for k_block in range(tiles_side):
                q_first = q_block * tile_length
                k_first = k_block * tile_length
                static_gap = distance * shard_len + q_first - k_first
                if static_gap + tile_length - 1 < 0:
                    continue
                if static_gap - (tile_length - 1) > reach_len - 1:
                    continue

                def compute(
                    inner_acc,
                    source=source,
                    key_start=key_start,
                    q_first=q_first,
                    k_first=k_first,
                    key_doc_tiles=key_doc_tiles,
                    key_span_tiles=key_span_tiles,
                    q_block=q_block,
                    k_block=k_block,
                ):
                    numer_in, denom_in = inner_acc
                    query_tile = grouped[q_first : q_first + tile_length]
                    kv_tile = source[k_first : k_first + tile_length]
                    scores = (
                        jnp.einsum(
                            "qhgd,khd->qhgk",
                            query_tile,
                            kv_tile[:, :, :HEAD_SIZE],
                            preferred_element_type=jnp.float32,
                        )
                        * inv_root
                    )
                    q_pos = query_start + q_first + offsets
                    k_pos = key_start + k_first + offsets
                    q_doc_t = query_doc_tiles[q_block]
                    q_span_t = query_span_tiles[q_block]
                    k_doc_t = key_doc_tiles[k_block]
                    k_span_t = key_span_tiles[k_block]
                    allowed = (
                        (q_doc_t[:, None] == k_doc_t[None, :])
                        & (q_span_t[:, None] == k_span_t[None, :])
                        & (k_pos[None, :] <= q_pos[:, None])
                    )
                    weights = jnp.where(allowed[:, None, None, :], jnp.exp(scores), 0.0)
                    part_den = jnp.sum(weights, axis=3)
                    part_num = jnp.einsum(
                        "qhgk,khd->qhgd",
                        weights.astype(jnp.bfloat16),
                        kv_tile[:, :, HEAD_SIZE:],
                        preferred_element_type=jnp.float32,
                    )
                    return (numer_in + part_num, denom_in + part_den)

                numer_list[q_block], denom_list[q_block] = lax.cond(
                    live_table[q_block, k_block],
                    compute,
                    lambda inner_acc: inner_acc,
                    (numer_list[q_block], denom_list[q_block]),
                )
    numerator = jnp.concatenate(numer_list, axis=0)
    denominator = jnp.concatenate(denom_list, axis=0)
    attended = (
        (numerator / denominator[..., None])
        .astype(jnp.bfloat16)
        .reshape(shard_len, local_heads, HEAD_SIZE)
    )
    returned = lax.all_to_all(attended, "exp", split_axis=0, concat_axis=1, tiled=True)
    return returned.reshape(shard_rows, QUERY_HEADS * HEAD_SIZE)


HALVES = 2
TAG_ROWS = 16


def unit_tile(tile):
    widened = tile.astype(jnp.float32)
    factor = lax.rsqrt(jnp.mean(widened * widened, axis=-1, keepdims=True) + 1e-06)
    return (widened * factor).astype(jnp.bfloat16)


def receive_order(lanes, z):
    late = int(z > 0)
    order = [(0, z)]
    for d in range(lanes + 1):
        e = d - late
        order += [(0, z + d + 1), (1, z + d), (0, z - d - 1)]
        order += [(1, z - e)] if e > 0 else []
        order += [(2, z + e)] if e >= 0 else []
    order += [(2, zp) for zp in range(lanes)]
    order = [(b, zp) for b, zp in order if 0 <= zp < lanes]
    return [b * lanes + zp for b, zp in dict.fromkeys(order)]


def relay_kernel(
    blocks, lanes, pairs, lent, q_ref, k_ref, v_ref, doc_ref, span_ref, out_ref,
    q_raw, k_raw, v_raw, id_raw, q_own, q_lent, kv, col, num, den, num_lent, den_lent, back,
    own_sem, recv_sem, send_sem, q_send, q_recv, back_send, back_recv,
):
    rows = k_ref.shape[0]
    top = lanes - 1
    ctx = lax.axis_index("ctx")
    z = lax.axis_index("exp")
    even = ctx % 2 == 0
    inner = (z >= 1) & (z < top)
    helper = (z == 1) | (z == top - 1)
    is_end = (z == 0) | (z == top)
    ward = jnp.where(z == 1, 0, top)
    mate = jnp.where(z == 0, 1, jnp.where(z == top, top - 1, ward))
    half_rows = 2 * rows
    pair_rows = HALVES * half_rows
    wide = HALVES * HEAD_SIZE
    count = 3 * lanes
    keepers = pairs - lent
    phases = []
    for i in range(max(lent, keepers)):
        phases += [i] if i < lent else []
        phases += [lent + i] if i < keepers else []
    tagged = (0, lent)

    barrier = pltpu.get_barrier_semaphore()
    neighbours = [
        (z > 0, (ctx, z - 1)), (z < top, (ctx, z + 1)),
        (ctx > 0, (ctx - 1, z)), (ctx < blocks - 1, (ctx + 1, z)),
        (even & (ctx > 1), (ctx - 2, z)), (even & (ctx < blocks - 2), (ctx + 2, z)),
    ]
    for present, device in neighbours:
        @pl.when(present)
        def _(device=device):
            pl.semaphore_signal(barrier, inc=1, device_id=device, device_id_type=MESH)

    loads = [
        pltpu.make_async_copy(ref, dst, own_sem.at[i])
        for i, (ref, dst) in enumerate(
            [(k_ref, k_raw), (v_ref, v_raw), (doc_ref, id_raw.at[pl.ds(0, 1)]), (span_ref, id_raw.at[pl.ds(1, 1)]), (q_ref, q_raw)]
        )
    ]
    for load in loads:
        load.start()
    num[...] = jnp.zeros_like(num)
    den[...] = jnp.zeros_like(den)
    num_lent[...] = jnp.zeros_like(num_lent)
    den_lent[...] = jnp.zeros_like(den_lent)
    for load in loads[:4]:
        load.wait()
    docs = jnp.broadcast_to(id_raw[0:1, :].astype(jnp.float32), (TAG_ROWS, rows))
    spans = jnp.broadcast_to(id_raw[1:2, :].astype(jnp.float32), (TAG_ROWS, rows))
    first = lax.broadcasted_iota(jnp.int32, (TAG_ROWS, rows), 0) == 0
    tags = jnp.where(first, docs, spans).astype(jnp.bfloat16)
    for p in range(pairs):
        for half in range(HALVES):
            column = (p * HALVES + half) * HEAD_SIZE
            kv[z, p, half * half_rows : half * half_rows + rows, :] = unit_tile(k_raw[:, column : column + HEAD_SIZE])
            kv[z, p, half * half_rows + rows : (half + 1) * half_rows, :] = v_raw[:, column : column + HEAD_SIZE]
        if p in tagged:
            kv[z, p, pair_rows : pair_rows + TAG_ROWS, :] = tags

    def code_of(slot, p):
        ids = kv[slot, p, pair_rows : pair_rows + TAG_ROWS, :].astype(jnp.float32)
        return jnp.broadcast_to(ids[0:1, :] * 256.0 + ids[1:2, :], (rows, rows))

    def set_column(which, slot, p):
        col[which] = code_of(slot, p).T

    pl.semaphore_wait(barrier, sum(present.astype(jnp.int32) for present, _ in neighbours))

    def routes(b, zp, p):
        if p < lent:
            up = ((b == 0) & (zp <= z) & (z < top - 1)) | ((b == 2) & (zp == 0) & (z == 0))
            down = (even & (b <= 1) & (zp >= z) & (z >= 2)) | (~even & (b == 0) & (zp == top) & (z == top))
            ctx1 = ((b == 0) & ((even & inner) | (~even & (zp <= z) & (ctx < blocks - 1) & (z >= 1)))) | (
                (b == 1) & even & inner & ((zp >= z) | (z == 1))
            )
            ctx2 = (b == 0) & even & (ctx < blocks - 2) & ((inner & (zp >= z)) | ((z == 0) & (zp == 0)))
        else:
            up = (b == 0) & (zp <= z) & (z < top)
            down = even & (b <= 1) & (zp >= z) & (z > 0)
            ctx1 = ((b == 0) & (even | ((zp <= z) & (ctx < blocks - 1)))) | ((b == 1) & even & (zp >= z))
            ctx2 = (b == 0) & even & (ctx < blocks - 2) & (zp >= z)
        slot = b * lanes + zp
        return [
            (0, up, (ctx, z + 1), slot),
            (1, down, (ctx, z - 1), slot),
            (2, ctx1, (ctx + 1, z), slot + lanes),
            (3, ctx2, (ctx + 2, z), slot + 2 * lanes),
        ]

    def arrives(b, zp, p):
        if p < lent:
            own_lane = ((b == 0) & ((zp < z) | ((zp > z) & (even | ((zp == top) & (z == top - 1)))))) | (
                (b == 1) & (ctx > 0)
            ) | ((b == 2) & (ctx > 1) & ((zp >= z) | ((z == 1) & (zp == 0))))
            return (inner & own_lane) | (
                (z == 0) & (b == 2) & (zp == 0) & even & (ctx > 1)
            ) | ((z == top) & (b == 1) & (zp == top) & even & (ctx > 0))
        return ((b == 0) & ((zp < z) | ((zp > z) & even))) | ((b == 1) & (ctx > 0)) | ((b == 2) & (ctx > 1) & (zp >= z))

    def piece(p, half):
        extra = TAG_ROWS if half == HALVES - 1 and p in tagged else 0
        return pl.ds(half * half_rows, half_rows + extra)

    def transfer(way, slot, p, half, device, to_slot):
        return pltpu.make_async_remote_copy(
            src_ref=kv.at[slot, p, piece(p, half)],
            dst_ref=kv.at[to_slot, p, piece(p, half)],
            send_sem=send_sem.at[way, slot, p],
            recv_sem=recv_sem.at[to_slot, p, half],
            device_id=device,
            device_id_type=MESH,
        )

    def forward(b, zp, p, halves, ways=(0, 1, 2, 3)):
        for way, taken, device, to_slot in routes(b, zp, p):
            if way in ways:
                @pl.when(taken)
                def _(way=way, device=device, to_slot=to_slot):
                    for half in halves:
                        transfer(way, b * lanes + zp, p, half, device, to_slot).start()

    def query_copy(p):
        return pltpu.make_async_remote_copy(
            src_ref=q_own.at[p], dst_ref=q_lent.at[p], send_sem=q_send.at[p], recv_sem=q_recv.at[p],
            device_id=(ctx, mate), device_id_type=MESH,
        )

    def back_copy(p, half):
        columns = pl.ds((p * HALVES + half) * GROUP * HEAD_SIZE, GROUP * HEAD_SIZE)
        return pltpu.make_async_remote_copy(
            src_ref=back.at[:, columns], dst_ref=out_ref.at[:, columns],
            send_sem=back_send.at[p, half], recv_sem=back_recv.at[p, half],
            device_id=(ctx, mate), device_id_type=MESH,
        )

    def unit_queries(p):
        for half in range(HALVES):
            for j in range(GROUP):
                column = ((p * HALVES + half) * GROUP + j) * HEAD_SIZE
                q_own[p, j * rows : (j + 1) * rows, half * HEAD_SIZE : (half + 1) * HEAD_SIZE] = unit_tile(
                    q_raw[:, column : column + HEAD_SIZE]
                )

    def send_own(i):
        if i < len(phases):
            p = phases[i]
            forward(0, z, p, range(HALVES))
            if p < lent:
                @pl.when(is_end)
                def _():
                    query_copy(p).start()

    scale = math.log2(math.e) * HEAD_SIZE ** (-0.5)

    def attend(slot, p, q_at, num_at, den_at, which, gap):
        tag = 0 if p < lent else lent
        code = code_of(slot, tag)
        own_code = col[which]
        ahead = lax.broadcasted_iota(jnp.int32, (rows, rows), 1) - lax.broadcasted_iota(jnp.int32, (rows, rows), 0)
        ahead = jnp.where(own_code == code, ahead, 1 << 20)
        kept = jnp.concatenate([ahead, ahead], axis=1) <= gap
        zeros = jnp.zeros((rows, HEAD_SIZE), jnp.bfloat16)

        def diagonal(start):
            return jnp.concatenate(
                [
                    jnp.concatenate([kv[slot, p, start : start + rows, :], zeros], axis=1),
                    jnp.concatenate([zeros, kv[slot, p, half_rows + start : half_rows + start + rows, :]], axis=1),
                ],
                axis=0,
            )

        scores = lax.dot_general(
            q_at[...], diagonal(0), (((1,), (1,)), ((), ())), preferred_element_type=jnp.float32
        )
        weights = [
            jnp.where(kept, jnp.exp2(scores[j * rows : (j + 1) * rows] * scale), 0.0) for j in range(GROUP)
        ]
        for j in range(GROUP):
            den_at[j * rows : (j + 1) * rows, :] += weights[j]
        packed = jnp.concatenate([w.astype(jnp.bfloat16) for w in weights], axis=0)
        num_at[...] += jnp.dot(packed, diagonal(rows), preferred_element_type=jnp.float32)

    def result(num_at, den_at, half, j):
        lane = slice(half * HEAD_SIZE, (half + 1) * HEAD_SIZE)
        row = slice(j * rows, (j + 1) * rows)
        total = jnp.sum(den_at[row, lane], axis=1, keepdims=True)
        return (num_at[row, lane] / total).astype(jnp.bfloat16)

    def finish(p, num_at, den_at, to, half):
        for j in range(GROUP):
            column = ((p * HALVES + half) * GROUP + j) * HEAD_SIZE
            to[:, column : column + HEAD_SIZE] = result(num_at, den_at, half, j)

    per_word = 6
    words = []
    for start in range(0, count, per_word):
        word = jnp.int32(0)
        for zz in range(lanes):
            entries = receive_order(lanes, zz)[start : start + per_word]
            word = jnp.where(z == zz, sum(s << (5 * i) for i, s in enumerate(entries)), word)
        words.append(word)

    def slot_of(k):
        word = words[0]
        for i in range(1, len(words)):
            word = jnp.where(k // per_word == i, words[i], word)
        return lax.shift_right_logical(word, 5 * (k % per_word)) & 31

    def drain(p):
        @pl.loop(0, count)
        def _(slot):
            b, zp = slot // lanes, slot % lanes
            here = arrives(b, zp, p) | (slot == z)
            for way, taken, device, to_slot in routes(b, zp, p):
                @pl.when(taken & here)
                def _(way=way, device=device, to_slot=to_slot):
                    whole = pl.ds(0, pair_rows + (TAG_ROWS if p in tagged else 0))
                    pltpu.make_async_remote_copy(
                        src_ref=kv.at[slot, p, whole], dst_ref=kv.at[to_slot, p, whole],
                        send_sem=send_sem.at[way, slot, p], recv_sem=recv_sem.at[to_slot, p, 0],
                        device_id=device, device_id_type=MESH,
                    ).wait_send()

    loads[4].wait()
    for p in range(lent):
        unit_queries(p)
    for i in range(AHEAD):
        send_own(i)
    for p in range(lent, pairs):
        unit_queries(p)
    set_column(0, z, 0)

    for i, p in enumerate(phases):
        if i > 0:
            send_own(i + AHEAD - 1)

        @pl.loop(0, count)
        def _(k, p=p):
            slot = slot_of(k)
            b, zp = slot // lanes, slot % lanes
            own = slot == z

            @pl.when(arrives(b, zp, p))
            def _():
                for half in range(HALVES):
                    transfer(0, slot, p, half, (ctx, z), slot).wait_recv()
                    forward(b, zp, p, (half,))

            needed = ((b == 0) & (zp <= z)) | ((b == 1) & (ctx > 0)) | ((b == 2) & (ctx > 1) & (zp >= z))
            if p < lent:
                needed = needed & inner

            @pl.when(needed)
            def _():
                attend(slot, p, q_own.at[p], num.at[p], den.at[p], 0, (b * lanes + z - zp) * rows)

        if p < lent:
            @pl.when(helper)
            def _(p=p):
                query_copy(p).wait_recv()
                if p == 0:
                    set_column(1, ward, 0)

                @pl.loop(0, count)
                def _(slot):
                    b, zp = slot // lanes, slot % lanes
                    needed = ((b == 0) & (zp <= ward)) | ((b == 1) & (ctx > 0)) | ((b == 2) & (ctx > 1) & (zp >= ward))

                    @pl.when(needed)
                    def _():
                        attend(slot, p, q_lent.at[p], num_lent.at[p], den_lent.at[p], 1, (b * lanes + ward - zp) * rows)

                for half in range(HALVES):
                    finish(p, num_lent.at[p], den_lent.at[p], back, half)
                    back_copy(p, half).start()

        @pl.when(inner if p < lent else z >= 0)
        def _(p=p):
            for half in range(HALVES):
                finish(p, num.at[p], den.at[p], out_ref, half)

        if i > 0:
            drain(phases[i - 1])
    drain(phases[-1])

    for p in range(lent):
        @pl.when(is_end)
        def _(p=p):
            query_copy(p).wait_send()
            for half in range(HALVES):
                back_copy(p, half).wait_recv()

        @pl.when(helper)
        def _(p=p):
            for half in range(HALVES):
                back_copy(p, half).wait_send()


AHEAD = 2


def relayed(queries, keys, values, doc_ids, span_ids):
    lanes = lax.axis_size("exp")
    blocks = lax.axis_size("ctx")
    rows = queries.shape[0]
    count = 3 * lanes
    pairs = KEY_VALUE_HEADS // HALVES
    lent = pairs // 2
    bf16, f32 = jnp.bfloat16, jnp.float32
    stack, wide = GROUP * rows, HALVES * HEAD_SIZE
    return pl.pallas_call(
        lambda *refs: relay_kernel(blocks, lanes, pairs, lent, *refs),
        out_shape=pltpu.VMEM(queries.shape, bf16),
        in_specs=[pl.BlockSpec(memory_space=pltpu.HBM)] * 5,
        out_specs=pl.BlockSpec(memory_space=pltpu.VMEM),
        scratch_shapes=[
            pltpu.VMEM(queries.shape, bf16),
            pltpu.VMEM(keys.shape, bf16),
            pltpu.VMEM(values.shape, bf16),
            pltpu.VMEM((2, rows), jnp.int32),
            pltpu.VMEM((pairs, stack, wide), bf16),
            pltpu.VMEM((lent, stack, wide), bf16),
            pltpu.VMEM((count, pairs, HALVES * 2 * rows + TAG_ROWS, HEAD_SIZE), bf16),
            pltpu.VMEM((2, rows, rows), f32),
            pltpu.VMEM((pairs, stack, wide), f32),
            pltpu.VMEM((pairs, stack, wide), f32),
            pltpu.VMEM((lent, stack, wide), f32),
            pltpu.VMEM((lent, stack, wide), f32),
            pltpu.VMEM((rows, lent * HALVES * GROUP * HEAD_SIZE), bf16),
            pltpu.SemaphoreType.DMA((5,)),
            pltpu.SemaphoreType.DMA((count, pairs, HALVES)),
            pltpu.SemaphoreType.DMA((4, count, pairs)),
            pltpu.SemaphoreType.DMA((lent,)),
            pltpu.SemaphoreType.DMA((lent,)),
            pltpu.SemaphoreType.DMA((lent, HALVES)),
            pltpu.SemaphoreType.DMA((lent, HALVES)),
        ],
        compiler_params=pltpu.CompilerParams(collective_id=0, has_side_effects=True, vmem_limit_bytes=60 << 20),
    )(queries, keys, values, doc_ids[None, :], span_ids[None, :])


def per_device(queries, keys, values, doc_ids, span_ids):
    lanes, blocks = lax.axis_size("exp"), lax.axis_size("ctx")
    rows = queries.shape[0]
    tokens = rows * lanes * blocks
    reach = min(SPAN, DOC_LEN if tokens > PACKED_TOKENS else DOC_TOP)
    if reach <= 2 * lanes * rows and blocks % 2 == 0 and 4 <= lanes <= 8 and rows == HEAD_SIZE:
        return relayed(queries, keys, values, doc_ids, span_ids)
    return general(queries, keys, values, doc_ids, span_ids)


def solution(mesh):
    in_specs = (
        P(("ctx", "exp"), None),
        P(("ctx", "exp"), None),
        P(("ctx", "exp"), None),
        P(("ctx", "exp")),
        P(("ctx", "exp")),
    )
    out_specs = P(("ctx", "exp"), None)
    return jax.shard_map(
        per_device, mesh=mesh, in_specs=in_specs, out_specs=out_specs, check_vma=False
    )
```

```python
import heapq
import math

import jax
import jax.numpy as jnp
from jax import lax
from jax.experimental import pallas as pl
from jax.experimental.pallas import tpu as pltpu
from jax.sharding import PartitionSpec as P

QUERY_HEADS = 32
KEY_VALUE_HEADS = 8
HEAD_SIZE = 128
SPAN = 8192
DOC_LEN = 2048
PACKED_TOKENS = 4096
DOC_TOP = 1024
GROUP = QUERY_HEADS // KEY_VALUE_HEADS
MESH = pl.DeviceIdType.MESH


def shifted(block, axis, distance):
    devices = range(lax.axis_size(axis))
    route = [(i - distance, i) for i in devices if i - distance in devices]
    return lax.ppermute(block, axis, route)


def single_unit_rows(tensor):
    widened = tensor.astype(jnp.float32)
    factor = lax.rsqrt(jnp.mean(widened * widened, axis=-1, keepdims=True) + 1e-06)
    return (widened * factor).astype(jnp.bfloat16)


def general(queries, keys, values, doc_ids, span_ids):
    expanded_size = lax.axis_size("exp")
    ctx_size = lax.axis_size("ctx")
    shard_rows = queries.shape[0]
    shard_len = shard_rows * expanded_size
    query_heads = single_unit_rows(queries.reshape(shard_rows, QUERY_HEADS, HEAD_SIZE))
    key_head_rows = single_unit_rows(keys.reshape(shard_rows, KEY_VALUE_HEADS, HEAD_SIZE))
    value_head_rows = values.reshape(shard_rows, KEY_VALUE_HEADS, HEAD_SIZE)
    head_replicas = max(1, expanded_size // KEY_VALUE_HEADS)
    reach_len = min(SPAN, DOC_LEN)
    steps_back = min((reach_len - 2) // shard_len + 1, ctx_size - 1)
    raw_pair = jnp.concatenate([key_head_rows, value_head_rows], axis=2)

    def spread(pair_rows):
        if head_replicas > 1:
            return jnp.repeat(pair_rows, head_replicas, axis=1)
        return pair_rows

    sources = []
    paired = spread(raw_pair)
    query_local, pair_local = (
        lax.all_to_all(query_heads, "exp", split_axis=1, concat_axis=0, tiled=True),
        lax.all_to_all(paired, "exp", split_axis=1, concat_axis=0, tiled=True),
    )
    block_doc, block_span = (
        lax.all_gather(doc_ids, "exp", axis=0, tiled=True),
        lax.all_gather(span_ids, "exp", axis=0, tiled=True),
    )
    sources.append((0, pair_local, block_doc, block_span))
    for distance in range(1, steps_back + 1):
        moved = shifted(pair_local, "ctx", distance)
        moved_doc, moved_span = shifted((block_doc, block_span), "ctx", distance)
        sources.append((distance, moved, moved_doc, moved_span))
    block_doc = sources[0][2]
    block_span = sources[0][3]
    local_heads = query_local.shape[1]
    pair_heads = sources[0][1].shape[1]
    query_group_width = local_heads // pair_heads
    ctx_index = lax.axis_index("ctx")
    tile_length = min(512, shard_len)
    tiles_side = shard_len // tile_length
    query_start = ctx_index * shard_len
    grouped = query_local.reshape(shard_len, pair_heads, query_group_width, HEAD_SIZE)
    inv_root = HEAD_SIZE ** (-0.5)
    offsets = jnp.arange(tile_length, dtype=jnp.int32)
    query_doc_tiles = block_doc.reshape(tiles_side, tile_length)
    query_span_tiles = block_span.reshape(tiles_side, tile_length)
    numer_list = [
        jnp.zeros((tile_length, pair_heads, query_group_width, HEAD_SIZE), jnp.float32)
        for _ in range(tiles_side)
    ]
    denom_list = [
        jnp.zeros((tile_length, pair_heads, query_group_width), jnp.float32)
        for _ in range(tiles_side)
    ]
    for distance, source, key_doc, key_span in sources:
        key_start = query_start - distance * shard_len
        present = ctx_index >= distance
        key_doc_tiles = key_doc.reshape(tiles_side, tile_length)
        key_span_tiles = key_span.reshape(tiles_side, tile_length)
        live_table = (
            (key_doc_tiles[None, :, tile_length - 1] >= query_doc_tiles[:, None, 0])
            & (key_span_tiles[None, :, tile_length - 1] >= query_span_tiles[:, None, 0])
            & present
        )
        for q_block in range(tiles_side):
            for k_block in range(tiles_side):
                q_first = q_block * tile_length
                k_first = k_block * tile_length
                static_gap = distance * shard_len + q_first - k_first
                if static_gap + tile_length - 1 < 0:
                    continue
                if static_gap - (tile_length - 1) > reach_len - 1:
                    continue

                def compute(
                    inner_acc,
                    source=source,
                    key_start=key_start,
                    q_first=q_first,
                    k_first=k_first,
                    key_doc_tiles=key_doc_tiles,
                    key_span_tiles=key_span_tiles,
                    q_block=q_block,
                    k_block=k_block,
                ):
                    numer_in, denom_in = inner_acc
                    query_tile = grouped[q_first : q_first + tile_length]
                    kv_tile = source[k_first : k_first + tile_length]
                    scores = (
                        jnp.einsum(
                            "qhgd,khd->qhgk",
                            query_tile,
                            kv_tile[:, :, :HEAD_SIZE],
                            preferred_element_type=jnp.float32,
                        )
                        * inv_root
                    )
                    q_pos = query_start + q_first + offsets
                    k_pos = key_start + k_first + offsets
                    q_doc_t = query_doc_tiles[q_block]
                    q_span_t = query_span_tiles[q_block]
                    k_doc_t = key_doc_tiles[k_block]
                    k_span_t = key_span_tiles[k_block]
                    allowed = (
                        (q_doc_t[:, None] == k_doc_t[None, :])
                        & (q_span_t[:, None] == k_span_t[None, :])
                        & (k_pos[None, :] <= q_pos[:, None])
                    )
                    weights = jnp.where(allowed[:, None, None, :], jnp.exp(scores), 0.0)
                    part_den = jnp.sum(weights, axis=3)
                    part_num = jnp.einsum(
                        "qhgk,khd->qhgd",
                        weights.astype(jnp.bfloat16),
                        kv_tile[:, :, HEAD_SIZE:],
                        preferred_element_type=jnp.float32,
                    )
                    return (numer_in + part_num, denom_in + part_den)

                numer_list[q_block], denom_list[q_block] = lax.cond(
                    live_table[q_block, k_block],
                    compute,
                    lambda inner_acc: inner_acc,
                    (numer_list[q_block], denom_list[q_block]),
                )
    numerator = jnp.concatenate(numer_list, axis=0)
    denominator = jnp.concatenate(denom_list, axis=0)
    attended = (
        (numerator / denominator[..., None])
        .astype(jnp.bfloat16)
        .reshape(shard_len, local_heads, HEAD_SIZE)
    )
    returned = lax.all_to_all(attended, "exp", split_axis=0, concat_axis=1, tiled=True)
    return returned.reshape(shard_rows, QUERY_HEADS * HEAD_SIZE)


def routes_of(ctx, z, b, zp, borrowed, blocks, lanes):
    top, even, inner = lanes - 1, ctx % 2 == 0, (z >= 1) & (z < lanes - 1)
    keep = (
        (b == 0) & (zp <= z) & (z < top),
        even & (b <= 1) & (zp >= z) & (z > 0),
        ((b == 0) & (even | ((zp <= z) & (ctx < blocks - 1)))) | ((b == 1) & even & (zp >= z)),
        (b == 0) & even & (ctx < blocks - 2) & (zp >= z),
    )
    lend = (
        ((b == 0) & (zp <= z) & (z < top - 1)) | ((b == 2) & (zp == 0) & (z == 0)),
        (even & (b <= 1) & (zp >= z) & (z >= 2)) | ((ctx % 2 == 1) & (b == 0) & (zp == top) & (z == top)),
        ((b == 0) & ((even & inner) | ((ctx % 2 == 1) & (zp <= z) & (ctx < blocks - 1) & (z >= 1))))
        | ((b == 1) & even & inner & ((zp >= z) | (z == 1))),
        (b == 0) & even & (ctx < blocks - 2) & ((inner & (zp >= z)) | ((z == 0) & (zp == 0))),
    )
    return [(borrowed & l) | ((borrowed ^ True) & k) for k, l in zip(keep, lend)]


def arrives_at(ctx, z, b, zp, borrowed, lanes):
    top, even, inner = lanes - 1, ctx % 2 == 0, (z >= 1) & (z < lanes - 1)
    before, two = (b == 1) & (ctx > 0), (b == 2) & (ctx > 1)
    keep = ((b == 0) & ((zp < z) | ((zp > z) & even))) | before | (two & (zp >= z))
    lend = (
        inner & (
            ((b == 0) & ((zp < z) | ((zp > z) & (even | ((zp == top) & (z == top - 1))))))
            | before | (two & ((zp >= z) | ((z == 1) & (zp == 0))))
        )
    ) | (even & (((z == 0) & two & (zp == 0)) | ((z == top) & before & (zp == top))))
    return (borrowed & lend) | ((borrowed ^ True) & keep)


def seen_from(ctx, z, b, zp):
    return ((b == 0) & (zp <= z)) | ((b == 1) & (ctx > 0)) | ((b == 2) & (ctx > 1) & (zp >= z))


WAIT, WAIT_TAGGED, ATTEND, TAKE, BACK, DONE = range(1, 7)


def plan(blocks, lanes, pairs, lent, knobs, halves=2, fixed=None):
    sequence, backlog, eager, cost = knobs
    hop, wire_time, inside, scalar, block, close = cost
    top = lanes - 1
    devices = [(c, z) for c in range(blocks) for z in range(lanes)]
    clock, events, log = 0, [], {d: [] for d in devices}
    queue, busy, q_parts = {}, {}, {}
    inbox = {d: [] for d in devices}
    got = {d: [] for d in devices}
    issued, at, part_at = dict.fromkeys(devices, 0), dict.fromkeys(devices, 0), dict.fromkeys(devices, 0)
    attended = {d: (set(), set()) for d in devices}
    closed = {d: set() for d in devices}
    idle = dict.fromkeys(devices, True)
    finish_at = dict.fromkeys(devices, 0.0)

    def ward_of(z):
        return 0 if z == 1 else top

    def push(t, kind, what):
        nonlocal clock
        clock += 1
        heapq.heappush(events, (t, clock, kind, what))

    def wire(d, way):
        c, z = d
        if way < 2:
            return ("z", c // 2, z, way)
        return ("in", c, z, 0) if way == 2 and c % 2 == 0 else ("c", c // 2, z, 0)

    def post(t, d, way, message):
        w = wire(d, way)
        queue.setdefault(w, {}).setdefault(d, []).append(message)
        if not busy.get(w):
            busy[w] = True
            push(t, "wire", (w, None))

    def send_slot(t, d, slot, p, parts):
        c, z = d
        b, zp = slot // lanes, slot % lanes
        to = ((c, z + 1, b), (c, z - 1, b), (c + 1, z, b + 1), (c + 2, z, b + 2))
        for way, taken in enumerate(routes_of(c, z, b, zp, p < lent, blocks, lanes)):
            if taken:
                for half in parts:
                    tc, tz, tb = to[way]
                    post(t, d, way, ((tc, tz), (tb * lanes + zp, p, half)))

    def issue(t, d, p):
        c, z = d
        send_slot(t, d, z, p, range(halves))
        if p < lent and z in (0, top):
            for i in range(2 * halves):
                post(t, d, 0 if z == 0 else 1, ((c, 1 if z == 0 else top - 1), (-1, p, i)))

    def give_back(t, d, p):
        for i in range(2 * halves):
            post(t + close, d, 1 if d[1] == 1 else 0, ((d[0], ward_of(d[1])), (-2, p, i)))

    def backlog_of(d, p):
        c, z = d
        used = [w for w, taken in enumerate(routes_of(c, z, 0, z, p < lent, blocks, lanes)) if taken]
        lens = [len(queue.get(wire(d, w), {}).get(d, [])) for w in used if not (w == 2 and c % 2 == 0)]
        if p < lent and z in (0, top):
            lens.append(len(queue.get(wire(d, 0 if z == 0 else 1), {}).get(d, [])))
        return min(lens) if lens else 0

    def wanted(d, target, p):
        c, z = d
        if p >= lent if target else (p < lent and z in (0, top)):
            return []
        return [s for s in range(3 * lanes) if seen_from(c, ward_of(z) if target else z, s // lanes, s % lanes)]

    def replay(t, d):
        c, z = d
        steps = fixed[(z, c % 2)]
        while at[d] < len(steps):
            kind, p, slot, other, target = steps[at[d]]
            b, zp = slot // lanes, slot % lanes
            at[d] += 1
            if kind == WAIT and slot == z:
                issue(t, d, p)
                return scalar
            if kind == WAIT and arrives_at(c, z, b, zp, p < lent, lanes):
                if any(m[1:] == (slot, p, part_at[d]) for m in inbox[d]):
                    send_slot(t + scalar / 2, d, slot, p, (part_at[d],))
                    part_at[d] = (part_at[d] + 1) % halves
                    at[d] -= part_at[d] > 0
                    return scalar
                at[d] -= 1
                return None
            if kind == TAKE and q_parts.get((d, p), 0) < 2 * halves:
                at[d] -= 1
                return None
            if kind == ATTEND and (slot // lanes <= c or other // lanes <= c):
                return scalar + block
            if kind == BACK:
                give_back(t, d, p)
            if kind in (BACK, DONE):
                return close
        return None

    def step(t, d):
        c, z = d
        ahead = eager[0] if z in (0, top) else eager[1]
        order = sequence[0] if z in (0, top) else sequence[1]
        if issued[d] < len(order) and issued[d] < ahead or (
            not inbox[d] and issued[d] < len(order) and backlog_of(d, order[issued[d]]) < backlog
        ):
            p = order[issued[d]]
            issued[d] += 1
            issue(t, d, p)
            got[d].append((z, p))
            log[d].append((WAIT, p, z, z, 0))
            return scalar
        if inbox[d]:
            _, slot, p, half = inbox[d].pop(0)
            send_slot(t + scalar / 2, d, slot, p, (half,))
            if half == halves - 1:
                got[d].append((slot, p))
                log[d].append((WAIT, p, slot, slot, 0))
            return scalar
        for target in (1, 0) if z in (1, top - 1) else (0,):
            for p in range(pairs):
                if target and (q_parts.get((d, p), 0) < 2 * halves or (ward_of(z), 0) not in got[d]):
                    continue
                todo = [s for s in wanted(d, target, p) if (s, p) not in attended[d][target]]
                tag = 0 if p < lent else lent
                ready = [s for s, q in got[d] if q == p and s in todo and (s, tag) in got[d]]
                if len(ready) > 1 or len(ready) == len(todo) == 1:
                    if target and ("q", p) not in closed[d]:
                        closed[d].add(("q", p))
                        log[d].append((TAKE, p, 0, 0, 1))
                    attended[d][target].update((s, p) for s in ready[:2])
                    log[d].append((ATTEND, p, ready[0], ready[min(1, len(ready) - 1)], target))
                    return scalar + block
                if not todo and wanted(d, target, p) and (target, p) not in closed[d]:
                    closed[d].add((target, p))
                    log[d].append((BACK if target else DONE, p, 0, 0, target))
                    if target:
                        give_back(t, d, p)
                    return close
        return None

    for d in devices:
        push(0.0, "go", d)
    while events:
        t, _, kind, what = heapq.heappop(events)
        if kind == "wire":
            w, last = what
            lines = [(d, q) for d, q in sorted(queue[w].items()) if q]
            if not lines:
                busy[w] = False
                continue
            d, q = ([x for x in lines if x[0] != last] or lines)[0]
            to, message = q.pop(0)
            length = inside if w[0] == "in" else wire_time
            push(t + length, "wire", (w, d))
            push(t + length + hop, "come", (to, message))
            wake = d
        elif kind == "come":
            wake, message = what
            finish_at[wake] = max(finish_at[wake], t)
            if message[0] >= 0:
                inbox[wake].append((t,) + message)
            elif message[0] == -1:
                q_parts[(wake, message[1])] = q_parts.get((wake, message[1]), 0) + 1
        else:
            length = (replay if fixed else step)(t, what)
            idle[what] = length is None
            if length is not None:
                finish_at[what] = max(finish_at[what], t + length)
                push(t + length, "go", what)
            continue
        if idle[wake]:
            idle[wake] = False
            push(t, "go", wake)
    if fixed:
        assert all(at[c, z] == len(fixed[z, c % 2]) for c, z in devices)
    return log, finish_at


def roles_of(log, blocks, lanes):
    middle = 2 * (blocks // 4)
    return {(z, parity): log[middle + parity, z] for z in range(lanes) for parity in range(2)}


HALVES = 2
TAG_ROWS = 16
LENT_PAIRS = 1
KNOBS = (([1, 2, 0, 3], [2, 3, 1, 0]), 1, (3, 4), (1.6, 1.45, 0.18, 0.1, 0.55, 0.4))
FAR = 1 << 20

PAIR_AT, SLOT_AT, OTHER_AT, FLAG_AT = 3, 6, 11, 16
OWN, QUERIES, FOR_WARD, ALONE = (1 << (FLAG_AT + i) for i in range(4))
WAY_AT = FLAG_AT + 4
SLOT_1, SLOT_2, OTHER_1, OTHER_2 = (1 << (WAY_AT + 4 + i) for i in range(4))


def unit_tile(tile):
    widened = tile.astype(jnp.float32)
    factor = lax.rsqrt(jnp.mean(widened * widened, axis=-1, keepdims=True) + 1e-06)
    return (widened * factor).astype(jnp.bfloat16)


def coded_steps(blocks, lanes, pairs, lent):
    roles = roles_of(plan(blocks, lanes, pairs, lent, KNOBS, 1)[0], blocks, lanes)
    coded = {}
    for (z, parity), steps in roles.items():
        ctx = 2 * (blocks // 4) + parity
        coded[z, parity] = []
        for kind, p, slot, other, target in steps:
            b, b2 = slot // lanes, other // lanes
            if kind == WAIT and p in (0, lent):
                kind = WAIT_TAGGED
            value = kind | p << PAIR_AT | slot << SLOT_AT | other << OTHER_AT | FOR_WARD * target
            value |= SLOT_1 * (b == 1) | SLOT_2 * (b == 2) | OTHER_1 * (b2 == 1) | OTHER_2 * (b2 == 2)
            if kind <= WAIT_TAGGED:
                ways = routes_of(ctx, z, b, slot % lanes, p < lent, blocks, lanes)
                value |= sum(int(taken) << (WAY_AT + way) for way, taken in enumerate(ways))
                value |= OWN * (slot == z)
                value |= QUERIES * (slot == z and p < lent and z in (0, lanes - 1))
            else:
                value |= ALONE * (slot == other)
            coded[z, parity].append(value)
    return coded


def sent_counts(blocks, lanes, pairs, lent):
    sent = [[[0] * (blocks * lanes) for _ in range(2)] for _ in range(4)]
    for ctx in range(blocks):
        for z in range(lanes):
            for slot in range(3 * lanes):
                for p in range(pairs):
                    b, zp = slot // lanes, slot % lanes
                    if slot == z or arrives_at(ctx, z, b, zp, p < lent, lanes):
                        for way, taken in enumerate(routes_of(ctx, z, b, zp, p < lent, blocks, lanes)):
                            sent[way][p in (0, lent)][ctx * lanes + z] += taken
    return sent


def relay_kernel(
    blocks, lanes, pairs, lent, steps, q_ref, k_ref, v_ref, doc_ref, span_ref, out_ref,
    q_raw, k_raw, v_raw, id_raw, q_unit, kv, col, acc, back, table,
    own_sem, recv_sem, send_sem, q_send, q_recv, back_send, back_recv,
):
    rows = k_ref.shape[0]
    top = lanes - 1
    ctx = lax.axis_index("ctx")
    z = lax.axis_index("exp")
    even = ctx % 2 == 0
    helper = (z == 1) | (z == top - 1)
    is_end = (z == 0) | (z == top)
    ward = jnp.where(z == 1, 0, top)
    mate = jnp.where(z == 0, 1, jnp.where(z == top, top - 1, ward))
    half_rows = 2 * rows
    pair_rows = HALVES * half_rows
    piece = pair_rows + TAG_ROWS
    length = max(len(s) for s in steps.values())
    sent = sent_counts(blocks, lanes, pairs, lent)

    barrier = pltpu.get_barrier_semaphore()
    neighbours = [
        (z > 0, (ctx, z - 1)), (z < top, (ctx, z + 1)),
        (ctx > 0, (ctx - 1, z)), (ctx < blocks - 1, (ctx + 1, z)),
        (even & (ctx > 1), (ctx - 2, z)), (even & (ctx < blocks - 2), (ctx + 2, z)),
    ]
    for present, device in neighbours:
        @pl.when(present)
        def _(device=device):
            pl.semaphore_signal(barrier, inc=1, device_id=device, device_id_type=MESH)

    loads = [
        pltpu.make_async_copy(ref, dst, own_sem.at[i])
        for i, (ref, dst) in enumerate(
            [(k_ref, k_raw), (v_ref, v_raw), (doc_ref, id_raw.at[pl.ds(0, 1)]), (span_ref, id_raw.at[pl.ds(1, 1)]), (q_ref, q_raw)]
        )
    ]
    for load in loads:
        load.start()

    role = z * 2 + ctx % 2
    lost_1 = jnp.where(ctx < 1, SLOT_1, 0) | jnp.where(ctx < 2, SLOT_2, 0)
    lost_2 = jnp.where(ctx < 1, OTHER_1, 0) | jnp.where(ctx < 2, OTHER_2, 0)
    shut = jnp.where(ctx == blocks - 1, 1 << (WAY_AT + 2), 0) | jnp.where(ctx >= blocks - 2, 1 << (WAY_AT + 3), 0)
    listed = {}
    own_length = jnp.int32(0)
    for (zz, parity), codes in steps.items():
        own_length = jnp.where(role == zz * 2 + parity, len(codes), own_length)
    for k in range(length):
        value = jnp.int32(0)
        for (zz, parity), codes in steps.items():
            if k < len(codes):
                value = jnp.where(role == zz * 2 + parity, codes[k], value)
        first_lost, second_lost = (value & lost_1) != 0, (value & lost_2) != 0
        waits = (value & 7) <= WAIT_TAGGED
        other = jnp.where(second_lost, value >> SLOT_AT, value >> OTHER_AT) & 31
        slot = jnp.where(first_lost, value >> OTHER_AT, value >> SLOT_AT) & 31
        fixed = (value & ~(1023 << SLOT_AT)) | slot << SLOT_AT | other << OTHER_AT
        fixed = fixed | jnp.where(first_lost | second_lost, ALONE, 0)
        fixed = jnp.where(first_lost & second_lost, 0, fixed)
        final = jnp.where(waits, jnp.where(first_lost, 0, value & ~shut), fixed)
        table[k] = final
        if any(k < len(codes) and codes[k] & 7 == ATTEND for codes in steps.values()):
            listed[k] = final

    acc[...] = jnp.zeros_like(acc)
    for load in loads[:4]:
        load.wait()
    docs = jnp.broadcast_to(id_raw[0:1, :].astype(jnp.float32), (TAG_ROWS, rows))
    spans = jnp.broadcast_to(id_raw[1:2, :].astype(jnp.float32), (TAG_ROWS, rows))
    first = lax.broadcasted_iota(jnp.int32, (TAG_ROWS, rows), 0) == 0
    tags = jnp.where(first, docs, spans).astype(jnp.bfloat16)
    for p in range(pairs):
        for half in range(HALVES):
            column = (p * HALVES + half) * HEAD_SIZE
            kv[z * pairs + p, half * half_rows : half * half_rows + rows, :] = unit_tile(k_raw[:, column : column + HEAD_SIZE])
            kv[z * pairs + p, half * half_rows + rows : (half + 1) * half_rows, :] = v_raw[:, column : column + HEAD_SIZE]
        if p in (0, lent):
            kv[z * pairs + p, pair_rows : pair_rows + TAG_ROWS, :] = tags

    def code_of(slot, p):
        ids = kv[slot * pairs + p, pair_rows : pair_rows + TAG_ROWS, :].astype(jnp.float32)
        return jnp.broadcast_to(ids[0:1, :] * 256.0 + ids[1:2, :], (rows, rows))

    loads[4].wait()
    for p in range(pairs):
        for half in range(HALVES):
            for j in range(GROUP):
                column = ((p * HALVES + half) * GROUP + j) * HEAD_SIZE
                q_unit[p, half, j * rows : (j + 1) * rows, :] = unit_tile(q_raw[:, column : column + HEAD_SIZE])
    col[0] = code_of(z, 0).T

    pl.semaphore_wait(barrier, sum(present.astype(jnp.int32) for present, _ in neighbours))

    def copy(way, slot, p, size, device, to_slot):
        return pltpu.make_async_remote_copy(
            src_ref=kv.at[slot * pairs + p, pl.ds(0, size)],
            dst_ref=kv.at[to_slot * pairs + p, pl.ds(0, size)],
            send_sem=send_sem.at[way, int(size > pair_rows)],
            recv_sem=recv_sem.at[to_slot, p],
            device_id=device,
            device_id_type=MESH,
        )

    def query_copy(p):
        return pltpu.make_async_remote_copy(
            src_ref=q_unit.at[p], dst_ref=q_unit.at[pairs + p], send_sem=q_send.at[p], recv_sem=q_recv.at[p],
            device_id=(ctx, mate), device_id_type=MESH,
        )

    def back_copy(p, half):
        columns = pl.ds((p * HALVES + half) * GROUP * HEAD_SIZE, GROUP * HEAD_SIZE)
        return pltpu.make_async_remote_copy(
            src_ref=back.at[:, columns], dst_ref=out_ref.at[:, columns],
            send_sem=back_send.at[p, half], recv_sem=back_recv.at[p, half],
            device_id=(ctx, mate), device_id_type=MESH,
        )

    scale = math.log2(math.e) * HEAD_SIZE ** (-0.5)

    def attend(step):
        p = (step >> PAIR_AT) & 7
        slots = [(step >> SLOT_AT) & 31, (step >> OTHER_AT) & 31]
        for_ward = (step & FOR_WARD) != 0
        which = jnp.where(for_ward, 1, 0)
        lane = jnp.where(for_ward, ward, z)
        at = jnp.where(for_ward, pairs + p, p)
        tag = jnp.where(p < lent, 0, lent)
        ahead = lax.broadcasted_iota(jnp.int32, (rows, rows), 1) - lax.broadcasted_iota(jnp.int32, (rows, rows), 0)
        kept = []
        for i, slot in enumerate(slots):
            gap = (2 * lanes * lax.div(slot, lanes) + lane - slot) * rows
            if i == 1:
                gap = jnp.where((step & ALONE) != 0, -FAR, gap)
            near = jnp.where(col[which] == code_of(slot, tag), ahead, FAR) <= gap
            kept.append(near.astype(jnp.float32).astype(jnp.bfloat16))
        kept = jnp.concatenate(kept, axis=1)
        ones = jnp.ones((2 * rows, HEAD_SIZE), jnp.bfloat16)
        for half in range(HALVES):
            start = half * half_rows
            keys = jnp.concatenate([kv[slot * pairs + p, start : start + rows, :] for slot in slots], axis=0)
            scores = lax.dot_general(
                q_unit[at, half], keys, (((1,), (1,)), ((), ())), preferred_element_type=jnp.float32
            )
            weights = jnp.exp2(scores * scale).astype(jnp.bfloat16)
            weights = jnp.concatenate([weights[j * rows : (j + 1) * rows] * kept for j in range(GROUP)], axis=0)
            values = jnp.concatenate([kv[slot * pairs + p, start + rows : start + half_rows, :] for slot in slots], axis=0)
            acc[at, half] += jnp.dot(
                weights, jnp.concatenate([values, ones], axis=1), preferred_element_type=jnp.float32
            )

    def finish(at, p, to):
        for half in range(HALVES):
            for j in range(GROUP):
                column = pl.multiple_of(((p * HALVES + half) * GROUP + j) * HEAD_SIZE, HEAD_SIZE)
                part = acc[at, half, j * rows : (j + 1) * rows, :]
                to[:, pl.ds(column, HEAD_SIZE)] = (part[:, :HEAD_SIZE] / part[:, HEAD_SIZE:]).astype(jnp.bfloat16)

    @pl.loop(0, own_length)
    def _(k):
        step = table[k]
        kind = step & 7
        p = (step >> PAIR_AT) & 7
        slot = (step >> SLOT_AT) & 31

        def pass_on(size):
            here = (step & OWN) != 0

            @pl.when(~here)
            def _():
                copy(0, slot, p, size, (ctx, z), slot).wait_recv()

            for way, device, shift in ((2, (ctx + 1, z), 1), (0, (ctx, z + 1), 0), (1, (ctx, z - 1), 0), (3, (ctx + 2, z), 2)):
                @pl.when((step & (1 << (WAY_AT + way))) != 0)
                def _(way=way, device=device, shift=shift):
                    copy(way, slot, p, size, device, slot + shift * lanes).start()

            @pl.when((step & QUERIES) != 0)
            def _():
                query_copy(p).start()

        @pl.when(kind <= WAIT_TAGGED)
        def _():
            @pl.when(kind == WAIT)
            def _():
                pass_on(pair_rows)

            @pl.when(kind == WAIT_TAGGED)
            def _():
                pass_on(piece)

        @pl.when(kind == ATTEND)
        def _():
            chosen = jnp.int32(0)
            for i, value in listed.items():
                chosen = jnp.where(k == i, value, chosen)
            attend(chosen)

        @pl.when(kind > ATTEND)
        def _():
            for own_p in range(pairs):
                @pl.when((kind == DONE) & (p == own_p))
                def _(own_p=own_p):
                    finish(own_p, own_p, out_ref)

            for own_p in range(lent):
                @pl.when((kind == TAKE) & (p == own_p))
                def _(own_p=own_p):
                    query_copy(own_p).wait_recv()
                    if own_p == 0:
                        col[1] = code_of(ward, 0).T

                @pl.when((kind == BACK) & (p == own_p))
                def _(own_p=own_p):
                    finish(pairs + own_p, own_p, back)
                    for half in range(HALVES):
                        back_copy(own_p, half).start()

    place = ctx * lanes + z
    for way in range(4):
        for tag in range(2):
            size = pair_rows + TAG_ROWS * tag
            for number in sorted(set(sent[way][tag]) - {0}):
                among = jnp.int32(0)
                for i, n in enumerate(sent[way][tag]):
                    among = among | jnp.where(place == i, 1, 0) if n == number else among

                @pl.when(among != 0)
                def _(way=way, tag=tag, size=size, number=number):
                    whole = kv.at[pl.ds(0, number), pl.ds(0, size)]
                    pltpu.make_async_remote_copy(
                        src_ref=whole, dst_ref=whole, send_sem=send_sem.at[way, tag], recv_sem=recv_sem.at[0, 0],
                        device_id=(ctx, z), device_id_type=MESH,
                    ).wait_send()

    for p in range(lent):
        @pl.when(is_end)
        def _(p=p):
            query_copy(p).wait_send()
            for half in range(HALVES):
                back_copy(p, half).wait_recv()

        @pl.when(helper)
        def _(p=p):
            for half in range(HALVES):
                back_copy(p, half).wait_send()


def relayed(queries, keys, values, doc_ids, span_ids):
    lanes = lax.axis_size("exp")
    blocks = lax.axis_size("ctx")
    rows = queries.shape[0]
    count = 3 * lanes
    pairs = KEY_VALUE_HEADS // HALVES
    lent = LENT_PAIRS
    steps = coded_steps(blocks, lanes, pairs, lent)
    length = max(len(s) for s in steps.values())
    bf16, f32 = jnp.bfloat16, jnp.float32
    stack = GROUP * rows
    return pl.pallas_call(
        lambda *refs: relay_kernel(blocks, lanes, pairs, lent, steps, *refs),
        out_shape=pltpu.VMEM(queries.shape, bf16),
        in_specs=[pl.BlockSpec(memory_space=pltpu.HBM)] * 5,
        out_specs=pl.BlockSpec(memory_space=pltpu.VMEM),
        scratch_shapes=[
            pltpu.VMEM(queries.shape, bf16),
            pltpu.VMEM(keys.shape, bf16),
            pltpu.VMEM(values.shape, bf16),
            pltpu.VMEM((2, rows), jnp.int32),
            pltpu.VMEM((pairs + lent, HALVES, stack, HEAD_SIZE), bf16),
            pltpu.VMEM((count * pairs, HALVES * 2 * rows + TAG_ROWS, HEAD_SIZE), bf16),
            pltpu.VMEM((2, rows, rows), f32),
            pltpu.VMEM((pairs + lent, HALVES, stack, 2 * HEAD_SIZE), f32),
            pltpu.VMEM((rows, lent * HALVES * GROUP * HEAD_SIZE), bf16),
            pltpu.SMEM((length,), jnp.int32),
            pltpu.SemaphoreType.DMA((5,)),
            pltpu.SemaphoreType.DMA((count, pairs)),
            pltpu.SemaphoreType.DMA((4, 2)),
            pltpu.SemaphoreType.DMA((lent,)),
            pltpu.SemaphoreType.DMA((lent,)),
            pltpu.SemaphoreType.DMA((lent, HALVES)),
            pltpu.SemaphoreType.DMA((lent, HALVES)),
        ],
        compiler_params=pltpu.CompilerParams(collective_id=0, has_side_effects=True, vmem_limit_bytes=60 << 20),
    )(queries, keys, values, doc_ids[None, :], span_ids[None, :])


def per_device(queries, keys, values, doc_ids, span_ids):
    lanes, blocks = lax.axis_size("exp"), lax.axis_size("ctx")
    rows = queries.shape[0]
    tokens = rows * lanes * blocks
    reach = min(SPAN, DOC_LEN if tokens > PACKED_TOKENS else DOC_TOP)
    if reach <= 2 * lanes * rows and blocks % 2 == 0 and blocks >= 6 and 4 <= lanes <= 8 and rows == HEAD_SIZE:
        return relayed(queries, keys, values, doc_ids, span_ids)
    return general(queries, keys, values, doc_ids, span_ids)


def solution(mesh):
    in_specs = (
        P(("ctx", "exp"), None),
        P(("ctx", "exp"), None),
        P(("ctx", "exp"), None),
        P(("ctx", "exp")),
        P(("ctx", "exp")),
    )
    out_specs = P(("ctx", "exp"), None)
    return jax.shard_map(
        per_device, mesh=mesh, in_specs=in_specs, out_specs=out_specs, check_vma=False
    )
```

```python
import heapq
import math

import jax
import jax.numpy as jnp
from jax import lax
from jax.experimental import pallas as pl
from jax.experimental.pallas import tpu as pltpu
from jax.sharding import PartitionSpec as P

QUERY_HEADS = 32
KEY_VALUE_HEADS = 8
HEAD_SIZE = 128
SPAN = 8192
DOC_LEN = 2048
PACKED_TOKENS = 4096
DOC_TOP = 1024
GROUP = QUERY_HEADS // KEY_VALUE_HEADS
MESH = pl.DeviceIdType.MESH


def shifted(block, axis, distance):
    devices = range(lax.axis_size(axis))
    route = [(i - distance, i) for i in devices if i - distance in devices]
    return lax.ppermute(block, axis, route)


def single_unit_rows(tensor):
    widened = tensor.astype(jnp.float32)
    factor = lax.rsqrt(jnp.mean(widened * widened, axis=-1, keepdims=True) + 1e-06)
    return (widened * factor).astype(jnp.bfloat16)


def general(queries, keys, values, doc_ids, span_ids):
    expanded_size = lax.axis_size("exp")
    ctx_size = lax.axis_size("ctx")
    shard_rows = queries.shape[0]
    shard_len = shard_rows * expanded_size
    query_heads = single_unit_rows(queries.reshape(shard_rows, QUERY_HEADS, HEAD_SIZE))
    key_head_rows = single_unit_rows(keys.reshape(shard_rows, KEY_VALUE_HEADS, HEAD_SIZE))
    value_head_rows = values.reshape(shard_rows, KEY_VALUE_HEADS, HEAD_SIZE)
    head_replicas = max(1, expanded_size // KEY_VALUE_HEADS)
    reach_len = min(SPAN, DOC_LEN)
    steps_back = min((reach_len - 2) // shard_len + 1, ctx_size - 1)
    raw_pair = jnp.concatenate([key_head_rows, value_head_rows], axis=2)

    def spread(pair_rows):
        if head_replicas > 1:
            return jnp.repeat(pair_rows, head_replicas, axis=1)
        return pair_rows

    sources = []
    paired = spread(raw_pair)
    query_local, pair_local = (
        lax.all_to_all(query_heads, "exp", split_axis=1, concat_axis=0, tiled=True),
        lax.all_to_all(paired, "exp", split_axis=1, concat_axis=0, tiled=True),
    )
    block_doc, block_span = (
        lax.all_gather(doc_ids, "exp", axis=0, tiled=True),
        lax.all_gather(span_ids, "exp", axis=0, tiled=True),
    )
    sources.append((0, pair_local, block_doc, block_span))
    for distance in range(1, steps_back + 1):
        moved = shifted(pair_local, "ctx", distance)
        moved_doc, moved_span = shifted((block_doc, block_span), "ctx", distance)
        sources.append((distance, moved, moved_doc, moved_span))
    block_doc = sources[0][2]
    block_span = sources[0][3]
    local_heads = query_local.shape[1]
    pair_heads = sources[0][1].shape[1]
    query_group_width = local_heads // pair_heads
    ctx_index = lax.axis_index("ctx")
    tile_length = min(512, shard_len)
    tiles_side = shard_len // tile_length
    query_start = ctx_index * shard_len
    grouped = query_local.reshape(shard_len, pair_heads, query_group_width, HEAD_SIZE)
    inv_root = HEAD_SIZE ** (-0.5)
    offsets = jnp.arange(tile_length, dtype=jnp.int32)
    query_doc_tiles = block_doc.reshape(tiles_side, tile_length)
    query_span_tiles = block_span.reshape(tiles_side, tile_length)
    numer_list = [
        jnp.zeros((tile_length, pair_heads, query_group_width, HEAD_SIZE), jnp.float32)
        for _ in range(tiles_side)
    ]
    denom_list = [
        jnp.zeros((tile_length, pair_heads, query_group_width), jnp.float32)
        for _ in range(tiles_side)
    ]
    for distance, source, key_doc, key_span in sources:
        key_start = query_start - distance * shard_len
        present = ctx_index >= distance
        key_doc_tiles = key_doc.reshape(tiles_side, tile_length)
        key_span_tiles = key_span.reshape(tiles_side, tile_length)
        live_table = (
            (key_doc_tiles[None, :, tile_length - 1] >= query_doc_tiles[:, None, 0])
            & (key_span_tiles[None, :, tile_length - 1] >= query_span_tiles[:, None, 0])
            & present
        )
        for q_block in range(tiles_side):
            for k_block in range(tiles_side):
                q_first = q_block * tile_length
                k_first = k_block * tile_length
                static_gap = distance * shard_len + q_first - k_first
                if static_gap + tile_length - 1 < 0:
                    continue
                if static_gap - (tile_length - 1) > reach_len - 1:
                    continue

                def compute(
                    inner_acc,
                    source=source,
                    key_start=key_start,
                    q_first=q_first,
                    k_first=k_first,
                    key_doc_tiles=key_doc_tiles,
                    key_span_tiles=key_span_tiles,
                    q_block=q_block,
                    k_block=k_block,
                ):
                    numer_in, denom_in = inner_acc
                    query_tile = grouped[q_first : q_first + tile_length]
                    kv_tile = source[k_first : k_first + tile_length]
                    scores = (
                        jnp.einsum(
                            "qhgd,khd->qhgk",
                            query_tile,
                            kv_tile[:, :, :HEAD_SIZE],
                            preferred_element_type=jnp.float32,
                        )
                        * inv_root
                    )
                    q_pos = query_start + q_first + offsets
                    k_pos = key_start + k_first + offsets
                    q_doc_t = query_doc_tiles[q_block]
                    q_span_t = query_span_tiles[q_block]
                    k_doc_t = key_doc_tiles[k_block]
                    k_span_t = key_span_tiles[k_block]
                    allowed = (
                        (q_doc_t[:, None] == k_doc_t[None, :])
                        & (q_span_t[:, None] == k_span_t[None, :])
                        & (k_pos[None, :] <= q_pos[:, None])
                    )
                    weights = jnp.where(allowed[:, None, None, :], jnp.exp(scores), 0.0)
                    part_den = jnp.sum(weights, axis=3)
                    part_num = jnp.einsum(
                        "qhgk,khd->qhgd",
                        weights.astype(jnp.bfloat16),
                        kv_tile[:, :, HEAD_SIZE:],
                        preferred_element_type=jnp.float32,
                    )
                    return (numer_in + part_num, denom_in + part_den)

                numer_list[q_block], denom_list[q_block] = lax.cond(
                    live_table[q_block, k_block],
                    compute,
                    lambda inner_acc: inner_acc,
                    (numer_list[q_block], denom_list[q_block]),
                )
    numerator = jnp.concatenate(numer_list, axis=0)
    denominator = jnp.concatenate(denom_list, axis=0)
    attended = (
        (numerator / denominator[..., None])
        .astype(jnp.bfloat16)
        .reshape(shard_len, local_heads, HEAD_SIZE)
    )
    returned = lax.all_to_all(attended, "exp", split_axis=0, concat_axis=1, tiled=True)
    return returned.reshape(shard_rows, QUERY_HEADS * HEAD_SIZE)


def routes_of(ctx, z, b, zp, borrowed, blocks, lanes):
    top, even, inner = lanes - 1, ctx % 2 == 0, (z >= 1) & (z < lanes - 1)
    keep = (
        (b == 0) & (zp <= z) & (z < top),
        even & (b <= 1) & (zp >= z) & (z > 0),
        ((b == 0) & (even | ((zp <= z) & (ctx < blocks - 1)))) | ((b == 1) & even & (zp >= z)),
        (b == 0) & even & (ctx < blocks - 2) & (zp >= z),
    )
    lend = (
        ((b == 0) & (zp <= z) & (z < top - 1)) | ((b == 2) & (zp == 0) & (z == 0)),
        (even & (b <= 1) & (zp >= z) & (z >= 2)) | ((ctx % 2 == 1) & (b == 0) & (zp == top) & (z == top)),
        ((b == 0) & ((even & inner) | ((ctx % 2 == 1) & (zp <= z) & (ctx < blocks - 1) & (z >= 1))))
        | ((b == 1) & even & inner & ((zp >= z) | (z == 1))),
        (b == 0) & even & (ctx < blocks - 2) & ((inner & (zp >= z)) | ((z == 0) & (zp == 0))),
    )
    return [(borrowed & l) | ((borrowed ^ True) & k) for k, l in zip(keep, lend)]


def arrives_at(ctx, z, b, zp, borrowed, lanes):
    top, even, inner = lanes - 1, ctx % 2 == 0, (z >= 1) & (z < lanes - 1)
    before, two = (b == 1) & (ctx > 0), (b == 2) & (ctx > 1)
    keep = ((b == 0) & ((zp < z) | ((zp > z) & even))) | before | (two & (zp >= z))
    lend = (
        inner & (
            ((b == 0) & ((zp < z) | ((zp > z) & (even | ((zp == top) & (z == top - 1))))))
            | before | (two & ((zp >= z) | ((z == 1) & (zp == 0))))
        )
    ) | (even & (((z == 0) & two & (zp == 0)) | ((z == top) & before & (zp == top))))
    return (borrowed & lend) | ((borrowed ^ True) & keep)


def seen_from(ctx, z, b, zp):
    return ((b == 0) & (zp <= z)) | ((b == 1) & (ctx > 0)) | ((b == 2) & (ctx > 1) & (zp >= z))


WAIT, WAIT_TAGGED, ATTEND, TAKE, BACK, DONE = range(1, 7)


def plan(blocks, lanes, pairs, lent, knobs, halves=2, fixed=None):
    sequence, backlog, eager, cost = knobs
    hop, wire_time, inside, scalar, block, close = cost
    top = lanes - 1
    devices = [(c, z) for c in range(blocks) for z in range(lanes)]
    clock, events, log = 0, [], {d: [] for d in devices}
    queue, busy, q_parts = {}, {}, {}
    inbox = {d: [] for d in devices}
    got = {d: [] for d in devices}
    issued, at, part_at = dict.fromkeys(devices, 0), dict.fromkeys(devices, 0), dict.fromkeys(devices, 0)
    attended = {d: (set(), set()) for d in devices}
    closed = {d: set() for d in devices}
    idle = dict.fromkeys(devices, True)
    finish_at = dict.fromkeys(devices, 0.0)

    def ward_of(z):
        return 0 if z == 1 else top

    def push(t, kind, what):
        nonlocal clock
        clock += 1
        heapq.heappush(events, (t, clock, kind, what))

    def wire(d, way):
        c, z = d
        if way < 2:
            return ("z", c // 2, z, way)
        return ("in", c, z, 0) if way == 2 and c % 2 == 0 else ("c", c // 2, z, 0)

    def post(t, d, way, message):
        w = wire(d, way)
        queue.setdefault(w, {}).setdefault(d, []).append(message)
        if not busy.get(w):
            busy[w] = True
            push(t, "wire", (w, None))

    def send_slot(t, d, slot, p, parts):
        c, z = d
        b, zp = slot // lanes, slot % lanes
        to = ((c, z + 1, b), (c, z - 1, b), (c + 1, z, b + 1), (c + 2, z, b + 2))
        for way, taken in enumerate(routes_of(c, z, b, zp, p < lent, blocks, lanes)):
            if taken:
                for half in parts:
                    tc, tz, tb = to[way]
                    post(t, d, way, ((tc, tz), (tb * lanes + zp, p, half)))

    def issue(t, d, p):
        c, z = d
        send_slot(t, d, z, p, range(halves))
        if p < lent and z in (0, top):
            for i in range(2 * halves):
                post(t, d, 0 if z == 0 else 1, ((c, 1 if z == 0 else top - 1), (-1, p, i)))

    def give_back(t, d, p):
        for i in range(2 * halves):
            post(t + close, d, 1 if d[1] == 1 else 0, ((d[0], ward_of(d[1])), (-2, p, i)))

    def backlog_of(d, p):
        c, z = d
        used = [w for w, taken in enumerate(routes_of(c, z, 0, z, p < lent, blocks, lanes)) if taken]
        lens = [len(queue.get(wire(d, w), {}).get(d, [])) for w in used if not (w == 2 and c % 2 == 0)]
        if p < lent and z in (0, top):
            lens.append(len(queue.get(wire(d, 0 if z == 0 else 1), {}).get(d, [])))
        return min(lens) if lens else 0

    def wanted(d, target, p):
        c, z = d
        if p >= lent if target else (p < lent and z in (0, top)):
            return []
        return [s for s in range(3 * lanes) if seen_from(c, ward_of(z) if target else z, s // lanes, s % lanes)]

    def replay(t, d):
        c, z = d
        steps = fixed[(z, c % 2)]
        while at[d] < len(steps):
            kind, p, slot, other, target = steps[at[d]]
            b, zp = slot // lanes, slot % lanes
            at[d] += 1
            if kind == WAIT and slot == z:
                issue(t, d, p)
                return scalar
            if kind == WAIT and arrives_at(c, z, b, zp, p < lent, lanes):
                if any(m[1:] == (slot, p, part_at[d]) for m in inbox[d]):
                    send_slot(t + scalar / 2, d, slot, p, (part_at[d],))
                    part_at[d] = (part_at[d] + 1) % halves
                    at[d] -= part_at[d] > 0
                    return scalar
                at[d] -= 1
                return None
            if kind == TAKE and q_parts.get((d, p), 0) < 2 * halves:
                at[d] -= 1
                return None
            if kind == ATTEND and (slot // lanes <= c or other // lanes <= c):
                return scalar + block
            if kind == BACK:
                give_back(t, d, p)
            if kind in (BACK, DONE):
                return close
        return None

    def step(t, d):
        c, z = d
        ahead = eager[0] if z in (0, top) else eager[1]
        order = sequence[0] if z in (0, top) else sequence[1]
        if issued[d] < len(order) and issued[d] < ahead or (
            not inbox[d] and issued[d] < len(order) and backlog_of(d, order[issued[d]]) < backlog
        ):
            p = order[issued[d]]
            issued[d] += 1
            issue(t, d, p)
            got[d].append((z, p))
            log[d].append((WAIT, p, z, z, 0))
            return scalar
        if inbox[d]:
            _, slot, p, half = inbox[d].pop(0)
            send_slot(t + scalar / 2, d, slot, p, (half,))
            if half == halves - 1:
                got[d].append((slot, p))
                log[d].append((WAIT, p, slot, slot, 0))
            return scalar
        for target in (1, 0) if z in (1, top - 1) else (0,):
            for p in range(pairs):
                if target and (q_parts.get((d, p), 0) < 2 * halves or (ward_of(z), 0) not in got[d]):
                    continue
                todo = [s for s in wanted(d, target, p) if (s, p) not in attended[d][target]]
                tag = 0 if p < lent else lent
                ready = [s for s, q in got[d] if q == p and s in todo and (s, tag) in got[d]]
                if len(ready) > 1 or len(ready) == len(todo) == 1:
                    if target and ("q", p) not in closed[d]:
                        closed[d].add(("q", p))
                        log[d].append((TAKE, p, 0, 0, 1))
                    attended[d][target].update((s, p) for s in ready[:2])
                    log[d].append((ATTEND, p, ready[0], ready[min(1, len(ready) - 1)], target))
                    return scalar + block
                if not todo and wanted(d, target, p) and (target, p) not in closed[d]:
                    closed[d].add((target, p))
                    log[d].append((BACK if target else DONE, p, 0, 0, target))
                    if target:
                        give_back(t, d, p)
                    return close
        return None

    for d in devices:
        push(0.0, "go", d)
    while events:
        t, _, kind, what = heapq.heappop(events)
        if kind == "wire":
            w, last = what
            lines = [(d, q) for d, q in sorted(queue[w].items()) if q]
            if not lines:
                busy[w] = False
                continue
            d, q = ([x for x in lines if x[0] != last] or lines)[0]
            to, message = q.pop(0)
            length = inside if w[0] == "in" else wire_time
            push(t + length, "wire", (w, d))
            push(t + length + hop, "come", (to, message))
            wake = d
        elif kind == "come":
            wake, message = what
            finish_at[wake] = max(finish_at[wake], t)
            if message[0] >= 0:
                inbox[wake].append((t,) + message)
            elif message[0] == -1:
                q_parts[(wake, message[1])] = q_parts.get((wake, message[1]), 0) + 1
        else:
            length = (replay if fixed else step)(t, what)
            idle[what] = length is None
            if length is not None:
                finish_at[what] = max(finish_at[what], t + length)
                push(t + length, "go", what)
            continue
        if idle[wake]:
            idle[wake] = False
            push(t, "go", wake)
    if fixed:
        assert all(at[c, z] == len(fixed[z, c % 2]) for c, z in devices)
    return log, finish_at


def roles_of(log, blocks, lanes):
    middle = 2 * (blocks // 4)
    return {(z, parity): log[middle + parity, z] for z in range(lanes) for parity in range(2)}


HALVES = 2
TAG_ROWS = 16
LENT_PAIRS = 1
KNOBS = (([1, 2, 0, 3], [1, 0, 3, 2]), 1, (2, 4), (2.0, 1.43, 0.18, 0.1, 0.3, 0.4))
FAR = 1 << 20

PAIR_AT, SLOT_AT, OTHER_AT, FLAG_AT = 3, 6, 11, 16
OWN, QUERIES, FOR_WARD, ALONE = (1 << (FLAG_AT + i) for i in range(4))
WAY_AT = FLAG_AT + 4
SLOT_1, SLOT_2, OTHER_1, OTHER_2 = (1 << (WAY_AT + 4 + i) for i in range(4))


def unit_tile(tile):
    widened = tile.astype(jnp.float32)
    factor = lax.rsqrt(jnp.mean(widened * widened, axis=-1, keepdims=True) + 1e-06)
    return (widened * factor).astype(jnp.bfloat16)


def coded_steps(blocks, lanes, pairs, lent):
    roles = roles_of(plan(blocks, lanes, pairs, lent, KNOBS, 1)[0], blocks, lanes)
    coded = {}
    for (z, parity), steps in roles.items():
        ctx = 2 * (blocks // 4) + parity
        coded[z, parity] = []
        for kind, p, slot, other, target in steps:
            b, b2 = slot // lanes, other // lanes
            if kind == WAIT and p in (0, lent):
                kind = WAIT_TAGGED
            value = kind | p << PAIR_AT | slot << SLOT_AT | other << OTHER_AT | FOR_WARD * target
            value |= SLOT_1 * (b == 1) | SLOT_2 * (b == 2) | OTHER_1 * (b2 == 1) | OTHER_2 * (b2 == 2)
            if kind <= WAIT_TAGGED:
                ways = routes_of(ctx, z, b, slot % lanes, p < lent, blocks, lanes)
                value |= sum(int(taken) << (WAY_AT + way) for way, taken in enumerate(ways))
                value |= OWN * (slot == z)
                value |= QUERIES * (slot == z and p < lent and z in (0, lanes - 1))
            else:
                value |= ALONE * (slot == other)
            coded[z, parity].append(value)
    return coded


def sent_counts(blocks, lanes, pairs, lent):
    sent = [[[0] * (blocks * lanes) for _ in range(2)] for _ in range(4)]
    for ctx in range(blocks):
        for z in range(lanes):
            for slot in range(3 * lanes):
                for p in range(pairs):
                    b, zp = slot // lanes, slot % lanes
                    if slot == z or arrives_at(ctx, z, b, zp, p < lent, lanes):
                        for way, taken in enumerate(routes_of(ctx, z, b, zp, p < lent, blocks, lanes)):
                            sent[way][p in (0, lent)][ctx * lanes + z] += taken
    return sent


def relay_kernel(
    blocks, lanes, pairs, lent, steps, q_ref, k_ref, v_ref, doc_ref, span_ref, out_ref,
    q_raw, k_raw, v_raw, id_raw, q_unit, kv, col, acc, back, table,
    own_sem, recv_sem, send_sem, q_send, q_recv, back_send, back_recv,
):
    rows = k_ref.shape[0]
    top = lanes - 1
    ctx = lax.axis_index("ctx")
    z = lax.axis_index("exp")
    even = ctx % 2 == 0
    helper = (z == 1) | (z == top - 1)
    is_end = (z == 0) | (z == top)
    ward = jnp.where(z == 1, 0, top)
    mate = jnp.where(z == 0, 1, jnp.where(z == top, top - 1, ward))
    half_rows = 2 * rows
    pair_rows = HALVES * half_rows
    piece = pair_rows + TAG_ROWS
    length = max(len(s) for s in steps.values())
    sent = sent_counts(blocks, lanes, pairs, lent)

    barrier = pltpu.get_barrier_semaphore()
    neighbours = [
        (z > 0, (ctx, z - 1)), (z < top, (ctx, z + 1)),
        (ctx > 0, (ctx - 1, z)), (ctx < blocks - 1, (ctx + 1, z)),
        (even & (ctx > 1), (ctx - 2, z)), (even & (ctx < blocks - 2), (ctx + 2, z)),
    ]
    for present, device in neighbours:
        @pl.when(present)
        def _(device=device):
            pl.semaphore_signal(barrier, inc=1, device_id=device, device_id_type=MESH)

    loads = [
        pltpu.make_async_copy(ref, dst, own_sem.at[i])
        for i, (ref, dst) in enumerate(
            [(k_ref, k_raw), (v_ref, v_raw), (doc_ref, id_raw.at[pl.ds(0, 1)]), (span_ref, id_raw.at[pl.ds(1, 1)]), (q_ref, q_raw)]
        )
    ]
    for load in loads:
        load.start()

    role = z * 2 + ctx % 2
    lost_1 = jnp.where(ctx < 1, SLOT_1, 0) | jnp.where(ctx < 2, SLOT_2, 0)
    lost_2 = jnp.where(ctx < 1, OTHER_1, 0) | jnp.where(ctx < 2, OTHER_2, 0)
    shut = jnp.where(ctx == blocks - 1, 1 << (WAY_AT + 2), 0) | jnp.where(ctx >= blocks - 2, 1 << (WAY_AT + 3), 0)
    listed = {}
    own_length = jnp.int32(0)
    for (zz, parity), codes in steps.items():
        own_length = jnp.where(role == zz * 2 + parity, len(codes), own_length)
    for k in range(length):
        value = jnp.int32(0)
        for (zz, parity), codes in steps.items():
            if k < len(codes):
                value = jnp.where(role == zz * 2 + parity, codes[k], value)
        first_lost, second_lost = (value & lost_1) != 0, (value & lost_2) != 0
        waits = (value & 7) <= WAIT_TAGGED
        other = jnp.where(second_lost, value >> SLOT_AT, value >> OTHER_AT) & 31
        slot = jnp.where(first_lost, value >> OTHER_AT, value >> SLOT_AT) & 31
        fixed = (value & ~(1023 << SLOT_AT)) | slot << SLOT_AT | other << OTHER_AT
        fixed = fixed | jnp.where(first_lost | second_lost, ALONE, 0)
        fixed = jnp.where(first_lost & second_lost, 0, fixed)
        final = jnp.where(waits, jnp.where(first_lost, 0, value & ~shut), fixed)
        table[k] = final
        if any(k < len(codes) and codes[k] & 7 == ATTEND for codes in steps.values()):
            listed[k] = final

    acc[...] = jnp.zeros_like(acc)
    for load in loads[:4]:
        load.wait()
    docs = jnp.broadcast_to(id_raw[0:1, :].astype(jnp.float32), (TAG_ROWS, rows))
    spans = jnp.broadcast_to(id_raw[1:2, :].astype(jnp.float32), (TAG_ROWS, rows))
    first = lax.broadcasted_iota(jnp.int32, (TAG_ROWS, rows), 0) == 0
    tags = jnp.where(first, docs, spans).astype(jnp.bfloat16)
    for p in range(pairs):
        for half in range(HALVES):
            column = (p * HALVES + half) * HEAD_SIZE
            kv[z * pairs + p, half * half_rows : half * half_rows + rows, :] = unit_tile(k_raw[:, column : column + HEAD_SIZE])
            kv[z * pairs + p, half * half_rows + rows : (half + 1) * half_rows, :] = v_raw[:, column : column + HEAD_SIZE]
        if p in (0, lent):
            kv[z * pairs + p, pair_rows : pair_rows + TAG_ROWS, :] = tags

    def code_of(slot, p):
        ids = kv[slot * pairs + p, pair_rows : pair_rows + TAG_ROWS, :].astype(jnp.float32)
        return jnp.broadcast_to(ids[0:1, :] * 256.0 + ids[1:2, :], (rows, rows))

    loads[4].wait()
    for p in range(pairs):
        for half in range(HALVES):
            for j in range(GROUP):
                column = ((p * HALVES + half) * GROUP + j) * HEAD_SIZE
                q_unit[p, half, j * rows : (j + 1) * rows, :] = unit_tile(q_raw[:, column : column + HEAD_SIZE])
    col[0] = code_of(z, 0).T

    pl.semaphore_wait(barrier, sum(present.astype(jnp.int32) for present, _ in neighbours))

    def copy(way, slot, p, size, device, to_slot):
        return pltpu.make_async_remote_copy(
            src_ref=kv.at[slot * pairs + p, pl.ds(0, size)],
            dst_ref=kv.at[to_slot * pairs + p, pl.ds(0, size)],
            send_sem=send_sem.at[way, int(size > pair_rows)],
            recv_sem=recv_sem.at[to_slot, p],
            device_id=device,
            device_id_type=MESH,
        )

    def query_copy(p):
        return pltpu.make_async_remote_copy(
            src_ref=q_unit.at[p], dst_ref=q_unit.at[pairs + p], send_sem=q_send.at[p], recv_sem=q_recv.at[p],
            device_id=(ctx, mate), device_id_type=MESH,
        )

    def back_copy(p, half):
        columns = pl.ds((p * HALVES + half) * GROUP * HEAD_SIZE, GROUP * HEAD_SIZE)
        return pltpu.make_async_remote_copy(
            src_ref=back.at[:, columns], dst_ref=out_ref.at[:, columns],
            send_sem=back_send.at[p, half], recv_sem=back_recv.at[p, half],
            device_id=(ctx, mate), device_id_type=MESH,
        )

    scale = math.log2(math.e) * HEAD_SIZE ** (-0.5)

    def attend(step):
        p = (step >> PAIR_AT) & 7
        slots = [(step >> SLOT_AT) & 31, (step >> OTHER_AT) & 31]
        for_ward = (step & FOR_WARD) != 0
        which = jnp.where(for_ward, 1, 0)
        lane = jnp.where(for_ward, ward, z)
        at = jnp.where(for_ward, pairs + p, p)
        tag = jnp.where(p < lent, 0, lent)
        ahead = lax.broadcasted_iota(jnp.int32, (rows, rows), 1) - lax.broadcasted_iota(jnp.int32, (rows, rows), 0)
        kept = []
        for i, slot in enumerate(slots):
            gap = (2 * lanes * lax.div(slot, lanes) + lane - slot) * rows
            if i == 1:
                gap = jnp.where((step & ALONE) != 0, -FAR, gap)
            near = jnp.where(col[which] == code_of(slot, tag), ahead, FAR) <= gap
            kept.append(near.astype(jnp.float32).astype(jnp.bfloat16))
        kept = jnp.concatenate(kept, axis=1)
        ones = jnp.ones((2 * rows, HEAD_SIZE), jnp.bfloat16)
        for half in range(HALVES):
            start = half * half_rows
            keys = jnp.concatenate([kv[slot * pairs + p, start : start + rows, :] for slot in slots], axis=0)
            scores = lax.dot_general(
                q_unit[at, half], keys, (((1,), (1,)), ((), ())), preferred_element_type=jnp.float32
            )
            weights = jnp.exp2(scores * scale).astype(jnp.bfloat16)
            weights = jnp.concatenate([weights[j * rows : (j + 1) * rows] * kept for j in range(GROUP)], axis=0)
            values = jnp.concatenate([kv[slot * pairs + p, start + rows : start + half_rows, :] for slot in slots], axis=0)
            acc[at, half] += jnp.dot(
                weights, jnp.concatenate([values, ones], axis=1), preferred_element_type=jnp.float32
            )

    def finish(at, p, to):
        for half in range(HALVES):
            for j in range(GROUP):
                column = pl.multiple_of(((p * HALVES + half) * GROUP + j) * HEAD_SIZE, HEAD_SIZE)
                part = acc[at, half, j * rows : (j + 1) * rows, :]
                to[:, pl.ds(column, HEAD_SIZE)] = (part[:, :HEAD_SIZE] / part[:, HEAD_SIZE:]).astype(jnp.bfloat16)

    @pl.loop(0, own_length)
    def _(k):
        step = table[k]
        kind = step & 7
        p = (step >> PAIR_AT) & 7
        slot = (step >> SLOT_AT) & 31

        def pass_on(size):
            here = (step & OWN) != 0

            @pl.when(~here)
            def _():
                copy(0, slot, p, size, (ctx, z), slot).wait_recv()

            for way, device, shift in ((2, (ctx + 1, z), 1), (0, (ctx, z + 1), 0), (1, (ctx, z - 1), 0), (3, (ctx + 2, z), 2)):
                @pl.when((step & (1 << (WAY_AT + way))) != 0)
                def _(way=way, device=device, shift=shift):
                    copy(way, slot, p, size, device, slot + shift * lanes).start()

            @pl.when((step & QUERIES) != 0)
            def _():
                query_copy(p).start()

        @pl.when(kind <= WAIT_TAGGED)
        def _():
            @pl.when(kind == WAIT)
            def _():
                pass_on(pair_rows)

            @pl.when(kind == WAIT_TAGGED)
            def _():
                pass_on(piece)

        @pl.when(kind == ATTEND)
        def _():
            chosen = jnp.int32(0)
            for i, value in listed.items():
                chosen = jnp.where(k == i, value, chosen)
            attend(chosen)

        @pl.when(kind > ATTEND)
        def _():
            for own_p in range(pairs):
                @pl.when((kind == DONE) & (p == own_p))
                def _(own_p=own_p):
                    finish(own_p, own_p, out_ref)

            for own_p in range(lent):
                @pl.when((kind == TAKE) & (p == own_p))
                def _(own_p=own_p):
                    query_copy(own_p).wait_recv()
                    if own_p == 0:
                        col[1] = code_of(ward, 0).T

                @pl.when((kind == BACK) & (p == own_p))
                def _(own_p=own_p):
                    finish(pairs + own_p, own_p, back)
                    for half in range(HALVES):
                        back_copy(own_p, half).start()

    place = ctx * lanes + z
    for way in range(4):
        for tag in range(2):
            size = pair_rows + TAG_ROWS * tag
            for number in sorted(set(sent[way][tag]) - {0}):
                among = jnp.int32(0)
                for i, n in enumerate(sent[way][tag]):
                    among = among | jnp.where(place == i, 1, 0) if n == number else among

                @pl.when(among != 0)
                def _(way=way, tag=tag, size=size, number=number):
                    whole = kv.at[pl.ds(0, number), pl.ds(0, size)]
                    pltpu.make_async_remote_copy(
                        src_ref=whole, dst_ref=whole, send_sem=send_sem.at[way, tag], recv_sem=recv_sem.at[0, 0],
                        device_id=(ctx, z), device_id_type=MESH,
                    ).wait_send()

    for p in range(lent):
        @pl.when(is_end)
        def _(p=p):
            query_copy(p).wait_send()
            for half in range(HALVES):
                back_copy(p, half).wait_recv()

        @pl.when(helper)
        def _(p=p):
            for half in range(HALVES):
                back_copy(p, half).wait_send()


def relayed(queries, keys, values, doc_ids, span_ids):
    lanes = lax.axis_size("exp")
    blocks = lax.axis_size("ctx")
    rows = queries.shape[0]
    count = 3 * lanes
    pairs = KEY_VALUE_HEADS // HALVES
    lent = LENT_PAIRS
    steps = coded_steps(blocks, lanes, pairs, lent)
    length = max(len(s) for s in steps.values())
    bf16, f32 = jnp.bfloat16, jnp.float32
    stack = GROUP * rows
    return pl.pallas_call(
        lambda *refs: relay_kernel(blocks, lanes, pairs, lent, steps, *refs),
        out_shape=pltpu.VMEM(queries.shape, bf16),
        in_specs=[pl.BlockSpec(memory_space=pltpu.HBM)] * 5,
        out_specs=pl.BlockSpec(memory_space=pltpu.VMEM),
        scratch_shapes=[
            pltpu.VMEM(queries.shape, bf16),
            pltpu.VMEM(keys.shape, bf16),
            pltpu.VMEM(values.shape, bf16),
            pltpu.VMEM((2, rows), jnp.int32),
            pltpu.VMEM((pairs + lent, HALVES, stack, HEAD_SIZE), bf16),
            pltpu.VMEM((count * pairs, HALVES * 2 * rows + TAG_ROWS, HEAD_SIZE), bf16),
            pltpu.VMEM((2, rows, rows), f32),
            pltpu.VMEM((pairs + lent, HALVES, stack, 2 * HEAD_SIZE), f32),
            pltpu.VMEM((rows, lent * HALVES * GROUP * HEAD_SIZE), bf16),
            pltpu.SMEM((length,), jnp.int32),
            pltpu.SemaphoreType.DMA((5,)),
            pltpu.SemaphoreType.DMA((count, pairs)),
            pltpu.SemaphoreType.DMA((4, 2)),
            pltpu.SemaphoreType.DMA((lent,)),
            pltpu.SemaphoreType.DMA((lent,)),
            pltpu.SemaphoreType.DMA((lent, HALVES)),
            pltpu.SemaphoreType.DMA((lent, HALVES)),
        ],
        compiler_params=pltpu.CompilerParams(collective_id=0, has_side_effects=True, vmem_limit_bytes=60 << 20),
    )(queries, keys, values, doc_ids[None, :], span_ids[None, :])


def per_device(queries, keys, values, doc_ids, span_ids):
    lanes, blocks = lax.axis_size("exp"), lax.axis_size("ctx")
    rows = queries.shape[0]
    tokens = rows * lanes * blocks
    reach = min(SPAN, DOC_LEN if tokens > PACKED_TOKENS else DOC_TOP)
    if reach <= 2 * lanes * rows and blocks % 2 == 0 and blocks >= 6 and 4 <= lanes <= 8 and rows == HEAD_SIZE:
        return relayed(queries, keys, values, doc_ids, span_ids)
    return general(queries, keys, values, doc_ids, span_ids)


def solution(mesh):
    in_specs = (
        P(("ctx", "exp"), None),
        P(("ctx", "exp"), None),
        P(("ctx", "exp"), None),
        P(("ctx", "exp")),
        P(("ctx", "exp")),
    )
    out_specs = P(("ctx", "exp"), None)
    return jax.shard_map(
        per_device, mesh=mesh, in_specs=in_specs, out_specs=out_specs, check_vma=False
    )
```

```python
import heapq
import math

import jax
import jax.numpy as jnp
from jax import lax
from jax.experimental import pallas as pl
from jax.experimental.pallas import tpu as pltpu
from jax.sharding import PartitionSpec as P

QUERY_HEADS = 32
KEY_VALUE_HEADS = 8
HEAD_SIZE = 128
SPAN = 8192
DOC_LEN = 2048
PACKED_TOKENS = 4096
DOC_TOP = 1024
GROUP = QUERY_HEADS // KEY_VALUE_HEADS
MESH = pl.DeviceIdType.MESH


def shifted(block, axis, distance):
    devices = range(lax.axis_size(axis))
    route = [(i - distance, i) for i in devices if i - distance in devices]
    return lax.ppermute(block, axis, route)


def single_unit_rows(tensor):
    widened = tensor.astype(jnp.float32)
    factor = lax.rsqrt(jnp.mean(widened * widened, axis=-1, keepdims=True) + 1e-06)
    return (widened * factor).astype(jnp.bfloat16)


def general(queries, keys, values, doc_ids, span_ids):
    expanded_size = lax.axis_size("exp")
    ctx_size = lax.axis_size("ctx")
    shard_rows = queries.shape[0]
    shard_len = shard_rows * expanded_size
    query_heads = single_unit_rows(queries.reshape(shard_rows, QUERY_HEADS, HEAD_SIZE))
    key_head_rows = single_unit_rows(keys.reshape(shard_rows, KEY_VALUE_HEADS, HEAD_SIZE))
    value_head_rows = values.reshape(shard_rows, KEY_VALUE_HEADS, HEAD_SIZE)
    head_replicas = max(1, expanded_size // KEY_VALUE_HEADS)
    reach_len = min(SPAN, DOC_LEN)
    steps_back = min((reach_len - 2) // shard_len + 1, ctx_size - 1)
    raw_pair = jnp.concatenate([key_head_rows, value_head_rows], axis=2)

    def spread(pair_rows):
        if head_replicas > 1:
            return jnp.repeat(pair_rows, head_replicas, axis=1)
        return pair_rows

    sources = []
    paired = spread(raw_pair)
    query_local, pair_local = (
        lax.all_to_all(query_heads, "exp", split_axis=1, concat_axis=0, tiled=True),
        lax.all_to_all(paired, "exp", split_axis=1, concat_axis=0, tiled=True),
    )
    block_doc, block_span = (
        lax.all_gather(doc_ids, "exp", axis=0, tiled=True),
        lax.all_gather(span_ids, "exp", axis=0, tiled=True),
    )
    sources.append((0, pair_local, block_doc, block_span))
    for distance in range(1, steps_back + 1):
        moved = shifted(pair_local, "ctx", distance)
        moved_doc, moved_span = shifted((block_doc, block_span), "ctx", distance)
        sources.append((distance, moved, moved_doc, moved_span))
    block_doc = sources[0][2]
    block_span = sources[0][3]
    local_heads = query_local.shape[1]
    pair_heads = sources[0][1].shape[1]
    query_group_width = local_heads // pair_heads
    ctx_index = lax.axis_index("ctx")
    tile_length = min(512, shard_len)
    tiles_side = shard_len // tile_length
    query_start = ctx_index * shard_len
    grouped = query_local.reshape(shard_len, pair_heads, query_group_width, HEAD_SIZE)
    inv_root = HEAD_SIZE ** (-0.5)
    offsets = jnp.arange(tile_length, dtype=jnp.int32)
    query_doc_tiles = block_doc.reshape(tiles_side, tile_length)
    query_span_tiles = block_span.reshape(tiles_side, tile_length)
    numer_list = [
        jnp.zeros((tile_length, pair_heads, query_group_width, HEAD_SIZE), jnp.float32)
        for _ in range(tiles_side)
    ]
    denom_list = [
        jnp.zeros((tile_length, pair_heads, query_group_width), jnp.float32)
        for _ in range(tiles_side)
    ]
    for distance, source, key_doc, key_span in sources:
        key_start = query_start - distance * shard_len
        present = ctx_index >= distance
        key_doc_tiles = key_doc.reshape(tiles_side, tile_length)
        key_span_tiles = key_span.reshape(tiles_side, tile_length)
        live_table = (
            (key_doc_tiles[None, :, tile_length - 1] >= query_doc_tiles[:, None, 0])
            & (key_span_tiles[None, :, tile_length - 1] >= query_span_tiles[:, None, 0])
            & present
        )
        for q_block in range(tiles_side):
            for k_block in range(tiles_side):
                q_first = q_block * tile_length
                k_first = k_block * tile_length
                static_gap = distance * shard_len + q_first - k_first
                if static_gap + tile_length - 1 < 0:
                    continue
                if static_gap - (tile_length - 1) > reach_len - 1:
                    continue

                def compute(
                    inner_acc,
                    source=source,
                    key_start=key_start,
                    q_first=q_first,
                    k_first=k_first,
                    key_doc_tiles=key_doc_tiles,
                    key_span_tiles=key_span_tiles,
                    q_block=q_block,
                    k_block=k_block,
                ):
                    numer_in, denom_in = inner_acc
                    query_tile = grouped[q_first : q_first + tile_length]
                    kv_tile = source[k_first : k_first + tile_length]
                    scores = (
                        jnp.einsum(
                            "qhgd,khd->qhgk",
                            query_tile,
                            kv_tile[:, :, :HEAD_SIZE],
                            preferred_element_type=jnp.float32,
                        )
                        * inv_root
                    )
                    q_pos = query_start + q_first + offsets
                    k_pos = key_start + k_first + offsets
                    q_doc_t = query_doc_tiles[q_block]
                    q_span_t = query_span_tiles[q_block]
                    k_doc_t = key_doc_tiles[k_block]
                    k_span_t = key_span_tiles[k_block]
                    allowed = (
                        (q_doc_t[:, None] == k_doc_t[None, :])
                        & (q_span_t[:, None] == k_span_t[None, :])
                        & (k_pos[None, :] <= q_pos[:, None])
                    )
                    weights = jnp.where(allowed[:, None, None, :], jnp.exp(scores), 0.0)
                    part_den = jnp.sum(weights, axis=3)
                    part_num = jnp.einsum(
                        "qhgk,khd->qhgd",
                        weights.astype(jnp.bfloat16),
                        kv_tile[:, :, HEAD_SIZE:],
                        preferred_element_type=jnp.float32,
                    )
                    return (numer_in + part_num, denom_in + part_den)

                numer_list[q_block], denom_list[q_block] = lax.cond(
                    live_table[q_block, k_block],
                    compute,
                    lambda inner_acc: inner_acc,
                    (numer_list[q_block], denom_list[q_block]),
                )
    numerator = jnp.concatenate(numer_list, axis=0)
    denominator = jnp.concatenate(denom_list, axis=0)
    attended = (
        (numerator / denominator[..., None])
        .astype(jnp.bfloat16)
        .reshape(shard_len, local_heads, HEAD_SIZE)
    )
    returned = lax.all_to_all(attended, "exp", split_axis=0, concat_axis=1, tiled=True)
    return returned.reshape(shard_rows, QUERY_HEADS * HEAD_SIZE)


def routes_of(ctx, z, b, zp, borrowed, blocks, lanes):
    top, even, inner = lanes - 1, ctx % 2 == 0, (z >= 1) & (z < lanes - 1)
    keep = (
        (b == 0) & (zp <= z) & (z < top),
        even & (b <= 1) & (zp >= z) & (z > 0),
        ((b == 0) & (even | ((zp <= z) & (ctx < blocks - 1)))) | ((b == 1) & even & (zp >= z)),
        (b == 0) & even & (ctx < blocks - 2) & (zp >= z),
    )
    lend = (
        ((b == 0) & (zp <= z) & (z < top - 1)) | ((b == 2) & (zp == 0) & (z == 0)),
        (even & (b <= 1) & (zp >= z) & (z >= 2)) | ((ctx % 2 == 1) & (b == 0) & (zp == top) & (z == top)),
        ((b == 0) & ((even & inner) | ((ctx % 2 == 1) & (zp <= z) & (ctx < blocks - 1) & (z >= 1))))
        | ((b == 1) & even & inner & ((zp >= z) | (z == 1))),
        (b == 0) & even & (ctx < blocks - 2) & ((inner & (zp >= z)) | ((z == 0) & (zp == 0))),
    )
    return [(borrowed & l) | ((borrowed ^ True) & k) for k, l in zip(keep, lend)]


def arrives_at(ctx, z, b, zp, borrowed, lanes):
    top, even, inner = lanes - 1, ctx % 2 == 0, (z >= 1) & (z < lanes - 1)
    before, two = (b == 1) & (ctx > 0), (b == 2) & (ctx > 1)
    keep = ((b == 0) & ((zp < z) | ((zp > z) & even))) | before | (two & (zp >= z))
    lend = (
        inner & (
            ((b == 0) & ((zp < z) | ((zp > z) & (even | ((zp == top) & (z == top - 1))))))
            | before | (two & ((zp >= z) | ((z == 1) & (zp == 0))))
        )
    ) | (even & (((z == 0) & two & (zp == 0)) | ((z == top) & before & (zp == top))))
    return (borrowed & lend) | ((borrowed ^ True) & keep)


def seen_from(ctx, z, b, zp):
    return ((b == 0) & (zp <= z)) | ((b == 1) & (ctx > 0)) | ((b == 2) & (ctx > 1) & (zp >= z))


WAIT, WAIT_TAGGED, ATTEND, TAKE, BACK, DONE = range(1, 7)


def plan(blocks, lanes, pairs, lent, knobs, halves=2, fixed=None):
    sequence, backlog, eager, cost = knobs
    hop, wire_time, inside, scalar, block, close = cost
    top = lanes - 1
    devices = [(c, z) for c in range(blocks) for z in range(lanes)]
    clock, events, log = 0, [], {d: [] for d in devices}
    queue, busy, q_parts = {}, {}, {}
    inbox = {d: [] for d in devices}
    got = {d: [] for d in devices}
    issued, at, part_at = dict.fromkeys(devices, 0), dict.fromkeys(devices, 0), dict.fromkeys(devices, 0)
    attended = {d: (set(), set()) for d in devices}
    closed = {d: set() for d in devices}
    idle = dict.fromkeys(devices, True)
    finish_at = dict.fromkeys(devices, 0.0)

    def ward_of(z):
        return 0 if z == 1 else top

    def push(t, kind, what):
        nonlocal clock
        clock += 1
        heapq.heappush(events, (t, clock, kind, what))

    def wire(d, way):
        c, z = d
        if way < 2:
            return ("z", c // 2, z, way)
        return ("in", c, z, 0) if way == 2 and c % 2 == 0 else ("c", c // 2, z, 0)

    def post(t, d, way, message):
        w = wire(d, way)
        queue.setdefault(w, {}).setdefault(d, []).append(message)
        if not busy.get(w):
            busy[w] = True
            push(t, "wire", (w, None))

    def send_slot(t, d, slot, p, parts):
        c, z = d
        b, zp = slot // lanes, slot % lanes
        to = ((c, z + 1, b), (c, z - 1, b), (c + 1, z, b + 1), (c + 2, z, b + 2))
        for way, taken in enumerate(routes_of(c, z, b, zp, p < lent, blocks, lanes)):
            if taken:
                for half in parts:
                    tc, tz, tb = to[way]
                    post(t, d, way, ((tc, tz), (tb * lanes + zp, p, half)))

    def issue(t, d, p):
        c, z = d
        send_slot(t, d, z, p, range(halves))
        if p < lent and z in (0, top):
            for i in range(2 * halves):
                post(t, d, 0 if z == 0 else 1, ((c, 1 if z == 0 else top - 1), (-1, p, i)))

    def give_back(t, d, p):
        for i in range(2 * halves):
            post(t + close, d, 1 if d[1] == 1 else 0, ((d[0], ward_of(d[1])), (-2, p, i)))

    def backlog_of(d, p):
        c, z = d
        used = [w for w, taken in enumerate(routes_of(c, z, 0, z, p < lent, blocks, lanes)) if taken]
        lens = [len(queue.get(wire(d, w), {}).get(d, [])) for w in used if not (w == 2 and c % 2 == 0)]
        if p < lent and z in (0, top):
            lens.append(len(queue.get(wire(d, 0 if z == 0 else 1), {}).get(d, [])))
        return min(lens) if lens else 0

    def wanted(d, target, p):
        c, z = d
        if p >= lent if target else (p < lent and z in (0, top)):
            return []
        return [s for s in range(3 * lanes) if seen_from(c, ward_of(z) if target else z, s // lanes, s % lanes)]

    def replay(t, d):
        c, z = d
        steps = fixed[(z, c % 2)]
        while at[d] < len(steps):
            kind, p, slot, other, target = steps[at[d]]
            b, zp = slot // lanes, slot % lanes
            at[d] += 1
            if kind == WAIT and slot == z:
                issue(t, d, p)
                return scalar
            if kind == WAIT and arrives_at(c, z, b, zp, p < lent, lanes):
                if any(m[1:] == (slot, p, part_at[d]) for m in inbox[d]):
                    send_slot(t + scalar / 2, d, slot, p, (part_at[d],))
                    part_at[d] = (part_at[d] + 1) % halves
                    at[d] -= part_at[d] > 0
                    return scalar
                at[d] -= 1
                return None
            if kind == TAKE and q_parts.get((d, p), 0) < 2 * halves:
                at[d] -= 1
                return None
            if kind == ATTEND and (slot // lanes <= c or other // lanes <= c):
                return scalar + block
            if kind == BACK:
                give_back(t, d, p)
            if kind in (BACK, DONE):
                return close
        return None

    def step(t, d):
        c, z = d
        ahead = eager[0] if z in (0, top) else eager[1]
        order = sequence[0] if z in (0, top) else sequence[1]
        if issued[d] < len(order) and issued[d] < ahead or (
            not inbox[d] and issued[d] < len(order) and backlog_of(d, order[issued[d]]) < backlog
        ):
            p = order[issued[d]]
            issued[d] += 1
            issue(t, d, p)
            got[d].append((z, p))
            log[d].append((WAIT, p, z, z, 0))
            return scalar
        if inbox[d]:
            _, slot, p, half = inbox[d].pop(0)
            send_slot(t + scalar / 2, d, slot, p, (half,))
            if half == halves - 1:
                got[d].append((slot, p))
                log[d].append((WAIT, p, slot, slot, 0))
            return scalar
        for target in (1, 0) if z in (1, top - 1) else (0,):
            for p in range(pairs):
                if target and (q_parts.get((d, p), 0) < 2 * halves or (ward_of(z), 0) not in got[d]):
                    continue
                todo = [s for s in wanted(d, target, p) if (s, p) not in attended[d][target]]
                tag = 0 if p < lent else lent
                ready = [s for s, q in got[d] if q == p and s in todo and (s, tag) in got[d]]
                if len(ready) > 1 or len(ready) == len(todo) == 1:
                    if target and ("q", p) not in closed[d]:
                        closed[d].add(("q", p))
                        log[d].append((TAKE, p, 0, 0, 1))
                    attended[d][target].update((s, p) for s in ready[:2])
                    log[d].append((ATTEND, p, ready[0], ready[min(1, len(ready) - 1)], target))
                    return scalar + block
                if not todo and wanted(d, target, p) and (target, p) not in closed[d]:
                    closed[d].add((target, p))
                    log[d].append((BACK if target else DONE, p, 0, 0, target))
                    if target:
                        give_back(t, d, p)
                    return close
        return None

    for d in devices:
        push(0.0, "go", d)
    while events:
        t, _, kind, what = heapq.heappop(events)
        if kind == "wire":
            w, last = what
            lines = [(d, q) for d, q in sorted(queue[w].items()) if q]
            if not lines:
                busy[w] = False
                continue
            d, q = ([x for x in lines if x[0] != last] or lines)[0]
            to, message = q.pop(0)
            length = inside if w[0] == "in" else wire_time
            push(t + length, "wire", (w, d))
            push(t + length + hop, "come", (to, message))
            wake = d
        elif kind == "come":
            wake, message = what
            finish_at[wake] = max(finish_at[wake], t)
            if message[0] >= 0:
                inbox[wake].append((t,) + message)
            elif message[0] == -1:
                q_parts[(wake, message[1])] = q_parts.get((wake, message[1]), 0) + 1
        else:
            length = (replay if fixed else step)(t, what)
            idle[what] = length is None
            if length is not None:
                finish_at[what] = max(finish_at[what], t + length)
                push(t + length, "go", what)
            continue
        if idle[wake]:
            idle[wake] = False
            push(t, "go", wake)
    if fixed:
        assert all(at[c, z] == len(fixed[z, c % 2]) for c, z in devices)
    return log, finish_at


def roles_of(log, blocks, lanes):
    middle = 2 * (blocks // 4)
    return {(z, parity): log[middle + parity, z] for z in range(lanes) for parity in range(2)}


HALVES = 2
TAG_ROWS = 16
LENT_PAIRS = 1
KNOBS = (([1, 2, 0, 3], [2, 3, 1, 0]), 1, (3, 4), (1.6, 1.45, 0.18, 0.1, 0.55, 0.4))
FAR = 1 << 20

PAIR_AT, SLOT_AT, OTHER_AT, FLAG_AT = 3, 6, 11, 16
OWN, QUERIES, FOR_WARD, ALONE = (1 << (FLAG_AT + i) for i in range(4))
WAY_AT = FLAG_AT + 4
SLOT_1, SLOT_2, OTHER_1, OTHER_2 = (1 << (WAY_AT + 4 + i) for i in range(4))


def unit_tile(tile):
    widened = tile.astype(jnp.float32)
    factor = lax.rsqrt(jnp.mean(widened * widened, axis=-1, keepdims=True) + 1e-06)
    return (widened * factor).astype(jnp.bfloat16)


def coded_steps(blocks, lanes, pairs, lent):
    roles = roles_of(plan(blocks, lanes, pairs, lent, KNOBS, 1)[0], blocks, lanes)
    coded = {}
    for (z, parity), steps in roles.items():
        ctx = 2 * (blocks // 4) + parity
        coded[z, parity] = []
        for kind, p, slot, other, target in steps:
            b, b2 = slot // lanes, other // lanes
            if kind == WAIT and p in (0, lent):
                kind = WAIT_TAGGED
            value = kind | p << PAIR_AT | slot << SLOT_AT | other << OTHER_AT | FOR_WARD * target
            value |= SLOT_1 * (b == 1) | SLOT_2 * (b == 2) | OTHER_1 * (b2 == 1) | OTHER_2 * (b2 == 2)
            if kind <= WAIT_TAGGED:
                ways = routes_of(ctx, z, b, slot % lanes, p < lent, blocks, lanes)
                value |= sum(int(taken) << (WAY_AT + way) for way, taken in enumerate(ways))
                value |= OWN * (slot == z)
                value |= QUERIES * (slot == z and p < lent and z in (0, lanes - 1))
            else:
                value |= ALONE * (slot == other)
            coded[z, parity].append(value)
    return coded


def sent_counts(blocks, lanes, pairs, lent):
    sent = [[[0] * (blocks * lanes) for _ in range(2)] for _ in range(4)]
    for ctx in range(blocks):
        for z in range(lanes):
            for slot in range(3 * lanes):
                for p in range(pairs):
                    b, zp = slot // lanes, slot % lanes
                    if slot == z or arrives_at(ctx, z, b, zp, p < lent, lanes):
                        for way, taken in enumerate(routes_of(ctx, z, b, zp, p < lent, blocks, lanes)):
                            sent[way][p in (0, lent)][ctx * lanes + z] += taken
    return sent


def relay_kernel(
    blocks, lanes, pairs, lent, steps, q_ref, k_ref, v_ref, doc_ref, span_ref, out_ref,
    q_raw, k_raw, v_raw, id_raw, q_unit, kv, col, acc, back, table,
    own_sem, recv_sem, send_sem, q_send, q_recv, back_send, back_recv,
):
    rows = k_ref.shape[0]
    top = lanes - 1
    ctx = lax.axis_index("ctx")
    z = lax.axis_index("exp")
    even = ctx % 2 == 0
    helper = (z == 1) | (z == top - 1)
    is_end = (z == 0) | (z == top)
    ward = jnp.where(z == 1, 0, top)
    mate = jnp.where(z == 0, 1, jnp.where(z == top, top - 1, ward))
    half_rows = 2 * rows
    pair_rows = HALVES * half_rows
    piece = pair_rows + TAG_ROWS
    length = max(len(s) for s in steps.values())
    sent = sent_counts(blocks, lanes, pairs, lent)

    barrier = pltpu.get_barrier_semaphore()
    neighbours = [
        (z > 0, (ctx, z - 1)), (z < top, (ctx, z + 1)),
        (ctx > 0, (ctx - 1, z)), (ctx < blocks - 1, (ctx + 1, z)),
        (even & (ctx > 1), (ctx - 2, z)), (even & (ctx < blocks - 2), (ctx + 2, z)),
    ]
    for present, device in neighbours:
        @pl.when(present)
        def _(device=device):
            pl.semaphore_signal(barrier, inc=1, device_id=device, device_id_type=MESH)

    loads = [
        pltpu.make_async_copy(ref, dst, own_sem.at[i])
        for i, (ref, dst) in enumerate(
            [(k_ref, k_raw), (v_ref, v_raw), (doc_ref, id_raw.at[pl.ds(0, 1)]), (span_ref, id_raw.at[pl.ds(1, 1)]), (q_ref, q_raw)]
        )
    ]
    for load in loads:
        load.start()

    role = z * 2 + ctx % 2
    lost_1 = jnp.where(ctx < 1, SLOT_1, 0) | jnp.where(ctx < 2, SLOT_2, 0)
    lost_2 = jnp.where(ctx < 1, OTHER_1, 0) | jnp.where(ctx < 2, OTHER_2, 0)
    shut = jnp.where(ctx == blocks - 1, 1 << (WAY_AT + 2), 0) | jnp.where(ctx >= blocks - 2, 1 << (WAY_AT + 3), 0)
    listed = {}
    own_length = jnp.int32(0)
    for (zz, parity), codes in steps.items():
        own_length = jnp.where(role == zz * 2 + parity, len(codes), own_length)
    for k in range(length):
        value = jnp.int32(0)
        for (zz, parity), codes in steps.items():
            if k < len(codes):
                value = jnp.where(role == zz * 2 + parity, codes[k], value)
        first_lost, second_lost = (value & lost_1) != 0, (value & lost_2) != 0
        waits = (value & 7) <= WAIT_TAGGED
        other = jnp.where(second_lost, value >> SLOT_AT, value >> OTHER_AT) & 31
        slot = jnp.where(first_lost, value >> OTHER_AT, value >> SLOT_AT) & 31
        fixed = (value & ~(1023 << SLOT_AT)) | slot << SLOT_AT | other << OTHER_AT
        fixed = fixed | jnp.where(first_lost | second_lost, ALONE, 0)
        fixed = jnp.where(first_lost & second_lost, 0, fixed)
        final = jnp.where(waits, jnp.where(first_lost, 0, value & ~shut), fixed)
        table[k] = final
        if any(k < len(codes) and codes[k] & 7 == ATTEND for codes in steps.values()):
            listed[k] = final

    place = ctx * lanes + z
    holds = [[jnp.int32(0)] * 2 for _ in range(4)]
    for way in range(4):
        for tag in range(2):
            for i, number in enumerate(sent[way][tag]):
                holds[way][tag] = jnp.where(place == i, number, holds[way][tag])
    acc[...] = jnp.zeros_like(acc)
    for load in loads[:4]:
        load.wait()
    docs = jnp.broadcast_to(id_raw[0:1, :].astype(jnp.float32), (TAG_ROWS, rows))
    spans = jnp.broadcast_to(id_raw[1:2, :].astype(jnp.float32), (TAG_ROWS, rows))
    first = lax.broadcasted_iota(jnp.int32, (TAG_ROWS, rows), 0) == 0
    tags = jnp.where(first, docs, spans).astype(jnp.bfloat16)
    for p in range(pairs):
        for half in range(HALVES):
            column = (p * HALVES + half) * HEAD_SIZE
            kv[z * pairs + p, half * half_rows : half * half_rows + rows, :] = unit_tile(k_raw[:, column : column + HEAD_SIZE])
            kv[z * pairs + p, half * half_rows + rows : (half + 1) * half_rows, :] = v_raw[:, column : column + HEAD_SIZE]
        if p in (0, lent):
            kv[z * pairs + p, pair_rows : pair_rows + TAG_ROWS, :] = tags

    def code_of(slot, p):
        ids = kv[slot * pairs + p, pair_rows : pair_rows + TAG_ROWS, :].astype(jnp.float32)
        return jnp.broadcast_to(ids[0:1, :] * 256.0 + ids[1:2, :], (rows, rows))

    loads[4].wait()
    for p in range(pairs):
        for half in range(HALVES):
            for j in range(GROUP):
                column = ((p * HALVES + half) * GROUP + j) * HEAD_SIZE
                q_unit[p, half, j * rows : (j + 1) * rows, :] = unit_tile(q_raw[:, column : column + HEAD_SIZE])
    col[0] = code_of(z, 0).T

    pl.semaphore_wait(barrier, sum(present.astype(jnp.int32) for present, _ in neighbours))

    def copy(way, slot, p, size, device, to_slot):
        return pltpu.make_async_remote_copy(
            src_ref=kv.at[slot * pairs + p, pl.ds(0, size)],
            dst_ref=kv.at[to_slot * pairs + p, pl.ds(0, size)],
            send_sem=send_sem.at[way, int(size > pair_rows)],
            recv_sem=recv_sem.at[to_slot, p],
            device_id=device,
            device_id_type=MESH,
        )

    def query_copy(p):
        return pltpu.make_async_remote_copy(
            src_ref=q_unit.at[p], dst_ref=q_unit.at[pairs + p], send_sem=q_send.at[p], recv_sem=q_recv.at[p],
            device_id=(ctx, mate), device_id_type=MESH,
        )

    def back_copy(p, half):
        columns = pl.ds((p * HALVES + half) * GROUP * HEAD_SIZE, GROUP * HEAD_SIZE)
        return pltpu.make_async_remote_copy(
            src_ref=back.at[:, columns], dst_ref=out_ref.at[:, columns],
            send_sem=back_send.at[p, half], recv_sem=back_recv.at[p, half],
            device_id=(ctx, mate), device_id_type=MESH,
        )

    scale = math.log2(math.e) * HEAD_SIZE ** (-0.5)

    def attend(step):
        p = (step >> PAIR_AT) & 7
        slots = [(step >> SLOT_AT) & 31, (step >> OTHER_AT) & 31]
        for_ward = (step & FOR_WARD) != 0
        which = jnp.where(for_ward, 1, 0)
        lane = jnp.where(for_ward, ward, z)
        at = jnp.where(for_ward, pairs + p, p)
        tag = jnp.where(p < lent, 0, lent)
        ahead = lax.broadcasted_iota(jnp.int32, (rows, rows), 1) - lax.broadcasted_iota(jnp.int32, (rows, rows), 0)
        kept = []
        for i, slot in enumerate(slots):
            gap = (2 * lanes * lax.div(slot, lanes) + lane - slot) * rows
            if i == 1:
                gap = jnp.where((step & ALONE) != 0, -FAR, gap)
            near = jnp.where(col[which] == code_of(slot, tag), ahead, FAR) <= gap
            kept.append(near.astype(jnp.float32).astype(jnp.bfloat16))
        kept = jnp.concatenate(kept, axis=1)
        ones = jnp.ones((2 * rows, HEAD_SIZE), jnp.bfloat16)
        for half in range(HALVES):
            start = half * half_rows
            keys = jnp.concatenate([kv[slot * pairs + p, start : start + rows, :] for slot in slots], axis=0)
            scores = lax.dot_general(
                q_unit[at, half], keys, (((1,), (1,)), ((), ())), preferred_element_type=jnp.float32
            )
            weights = jnp.exp2(scores * scale).astype(jnp.bfloat16)
            weights = jnp.concatenate([weights[j * rows : (j + 1) * rows] * kept for j in range(GROUP)], axis=0)
            values = jnp.concatenate([kv[slot * pairs + p, start + rows : start + half_rows, :] for slot in slots], axis=0)
            acc[at, half] += jnp.dot(
                weights, jnp.concatenate([values, ones], axis=1), preferred_element_type=jnp.float32
            )

    def finish(at, p, to, halves=range(HALVES)):
        for half in halves:
            for j in range(GROUP):
                column = pl.multiple_of(((p * HALVES + half) * GROUP + j) * HEAD_SIZE, HEAD_SIZE)
                part = acc[at, half, j * rows : (j + 1) * rows, :]
                to[:, pl.ds(column, HEAD_SIZE)] = (part[:, :HEAD_SIZE] / part[:, HEAD_SIZE:]).astype(jnp.bfloat16)

    @pl.loop(0, own_length)
    def _(k):
        step = table[k]
        kind = step & 7
        p = (step >> PAIR_AT) & 7
        slot = (step >> SLOT_AT) & 31

        def pass_on(size):
            here = (step & OWN) != 0

            @pl.when(~here)
            def _():
                copy(0, slot, p, size, (ctx, z), slot).wait_recv()

            for way, device, shift in ((0, (ctx, z + 1), 0), (1, (ctx, z - 1), 0), (3, (ctx + 2, z), 2), (2, (ctx + 1, z), 1)):
                @pl.when((step & (1 << (WAY_AT + way))) != 0)
                def _(way=way, device=device, shift=shift):
                    copy(way, slot, p, size, device, slot + shift * lanes).start()

            @pl.when((step & QUERIES) != 0)
            def _():
                query_copy(p).start()

        @pl.when(kind <= WAIT_TAGGED)
        def _():
            @pl.when(kind == WAIT)
            def _():
                pass_on(pair_rows)

            @pl.when(kind == WAIT_TAGGED)
            def _():
                pass_on(piece)

        @pl.when(kind == ATTEND)
        def _():
            chosen = jnp.int32(0)
            for i, value in listed.items():
                chosen = jnp.where(k == i, value, chosen)
            attend(chosen)

        @pl.when(kind > ATTEND)
        def _():
            for own_p in range(pairs):
                @pl.when((kind == DONE) & (p == own_p))
                def _(own_p=own_p):
                    finish(own_p, own_p, out_ref)

            for own_p in range(lent):
                @pl.when((kind == TAKE) & (p == own_p))
                def _(own_p=own_p):
                    query_copy(own_p).wait_recv()
                    if own_p == 0:
                        col[1] = code_of(ward, 0).T

                @pl.when((kind == BACK) & (p == own_p))
                def _(own_p=own_p):
                    for half in range(HALVES):
                        finish(pairs + own_p, own_p, back, (half,))
                        back_copy(own_p, half).start()

    for way in range(4):
        for tag in range(2):
            size = pair_rows + TAG_ROWS * tag
            for number in sorted(set(sent[way][tag]) - {0}):
                @pl.when(holds[way][tag] == number)
                def _(way=way, tag=tag, size=size, number=number):
                    whole = kv.at[pl.ds(0, number), pl.ds(0, size)]
                    pltpu.make_async_remote_copy(
                        src_ref=whole, dst_ref=whole, send_sem=send_sem.at[way, tag], recv_sem=recv_sem.at[0, 0],
                        device_id=(ctx, z), device_id_type=MESH,
                    ).wait_send()

    for p in range(lent):
        @pl.when(is_end)
        def _(p=p):
            query_copy(p).wait_send()
            for half in range(HALVES):
                back_copy(p, half).wait_recv()

        @pl.when(helper)
        def _(p=p):
            for half in range(HALVES):
                back_copy(p, half).wait_send()


def relayed(queries, keys, values, doc_ids, span_ids):
    lanes = lax.axis_size("exp")
    blocks = lax.axis_size("ctx")
    rows = queries.shape[0]
    count = 3 * lanes
    pairs = KEY_VALUE_HEADS // HALVES
    lent = LENT_PAIRS
    steps = coded_steps(blocks, lanes, pairs, lent)
    length = max(len(s) for s in steps.values())
    bf16, f32 = jnp.bfloat16, jnp.float32
    stack = GROUP * rows
    return pl.pallas_call(
        lambda *refs: relay_kernel(blocks, lanes, pairs, lent, steps, *refs),
        out_shape=pltpu.VMEM(queries.shape, bf16),
        in_specs=[pl.BlockSpec(memory_space=pltpu.HBM)] * 5,
        out_specs=pl.BlockSpec(memory_space=pltpu.VMEM),
        scratch_shapes=[
            pltpu.VMEM(queries.shape, bf16),
            pltpu.VMEM(keys.shape, bf16),
            pltpu.VMEM(values.shape, bf16),
            pltpu.VMEM((2, rows), jnp.int32),
            pltpu.VMEM((pairs + lent, HALVES, stack, HEAD_SIZE), bf16),
            pltpu.VMEM((count * pairs, HALVES * 2 * rows + TAG_ROWS, HEAD_SIZE), bf16),
            pltpu.VMEM((2, rows, rows), f32),
            pltpu.VMEM((pairs + lent, HALVES, stack, 2 * HEAD_SIZE), f32),
            pltpu.VMEM((rows, lent * HALVES * GROUP * HEAD_SIZE), bf16),
            pltpu.SMEM((length,), jnp.int32),
            pltpu.SemaphoreType.DMA((5,)),
            pltpu.SemaphoreType.DMA((count, pairs)),
            pltpu.SemaphoreType.DMA((4, 2)),
            pltpu.SemaphoreType.DMA((lent,)),
            pltpu.SemaphoreType.DMA((lent,)),
            pltpu.SemaphoreType.DMA((lent, HALVES)),
            pltpu.SemaphoreType.DMA((lent, HALVES)),
        ],
        compiler_params=pltpu.CompilerParams(collective_id=0, has_side_effects=True, vmem_limit_bytes=60 << 20),
    )(queries, keys, values, doc_ids[None, :], span_ids[None, :])


def per_device(queries, keys, values, doc_ids, span_ids):
    lanes, blocks = lax.axis_size("exp"), lax.axis_size("ctx")
    rows = queries.shape[0]
    tokens = rows * lanes * blocks
    reach = min(SPAN, DOC_LEN if tokens > PACKED_TOKENS else DOC_TOP)
    if reach <= 2 * lanes * rows and blocks % 2 == 0 and blocks >= 6 and 4 <= lanes <= 8 and rows == HEAD_SIZE:
        return relayed(queries, keys, values, doc_ids, span_ids)
    return general(queries, keys, values, doc_ids, span_ids)


def solution(mesh):
    in_specs = (
        P(("ctx", "exp"), None),
        P(("ctx", "exp"), None),
        P(("ctx", "exp"), None),
        P(("ctx", "exp")),
        P(("ctx", "exp")),
    )
    out_specs = P(("ctx", "exp"), None)
    return jax.shard_map(
        per_device, mesh=mesh, in_specs=in_specs, out_specs=out_specs, check_vma=False
    )
```

```python
import heapq
import math

import jax
import jax.numpy as jnp
from jax import lax
from jax.experimental import pallas as pl
from jax.experimental.pallas import tpu as pltpu
from jax.sharding import PartitionSpec as P

QUERY_HEADS = 32
KEY_VALUE_HEADS = 8
HEAD_SIZE = 128
SPAN = 8192
DOC_LEN = 2048
PACKED_TOKENS = 4096
DOC_TOP = 1024
GROUP = QUERY_HEADS // KEY_VALUE_HEADS
MESH = pl.DeviceIdType.MESH


def shifted(block, axis, distance):
    devices = range(lax.axis_size(axis))
    route = [(i - distance, i) for i in devices if i - distance in devices]
    return lax.ppermute(block, axis, route)


def single_unit_rows(tensor):
    widened = tensor.astype(jnp.float32)
    factor = lax.rsqrt(jnp.mean(widened * widened, axis=-1, keepdims=True) + 1e-06)
    return (widened * factor).astype(jnp.bfloat16)


def general(queries, keys, values, doc_ids, span_ids):
    expanded_size = lax.axis_size("exp")
    ctx_size = lax.axis_size("ctx")
    shard_rows = queries.shape[0]
    shard_len = shard_rows * expanded_size
    query_heads = single_unit_rows(queries.reshape(shard_rows, QUERY_HEADS, HEAD_SIZE))
    key_head_rows = single_unit_rows(keys.reshape(shard_rows, KEY_VALUE_HEADS, HEAD_SIZE))
    value_head_rows = values.reshape(shard_rows, KEY_VALUE_HEADS, HEAD_SIZE)
    head_replicas = max(1, expanded_size // KEY_VALUE_HEADS)
    reach_len = min(SPAN, DOC_LEN)
    steps_back = min((reach_len - 2) // shard_len + 1, ctx_size - 1)
    raw_pair = jnp.concatenate([key_head_rows, value_head_rows], axis=2)

    def spread(pair_rows):
        if head_replicas > 1:
            return jnp.repeat(pair_rows, head_replicas, axis=1)
        return pair_rows

    sources = []
    paired = spread(raw_pair)
    query_local, pair_local = (
        lax.all_to_all(query_heads, "exp", split_axis=1, concat_axis=0, tiled=True),
        lax.all_to_all(paired, "exp", split_axis=1, concat_axis=0, tiled=True),
    )
    block_doc, block_span = (
        lax.all_gather(doc_ids, "exp", axis=0, tiled=True),
        lax.all_gather(span_ids, "exp", axis=0, tiled=True),
    )
    sources.append((0, pair_local, block_doc, block_span))
    for distance in range(1, steps_back + 1):
        moved = shifted(pair_local, "ctx", distance)
        moved_doc, moved_span = shifted((block_doc, block_span), "ctx", distance)
        sources.append((distance, moved, moved_doc, moved_span))
    block_doc = sources[0][2]
    block_span = sources[0][3]
    local_heads = query_local.shape[1]
    pair_heads = sources[0][1].shape[1]
    query_group_width = local_heads // pair_heads
    ctx_index = lax.axis_index("ctx")
    tile_length = min(512, shard_len)
    tiles_side = shard_len // tile_length
    query_start = ctx_index * shard_len
    grouped = query_local.reshape(shard_len, pair_heads, query_group_width, HEAD_SIZE)
    inv_root = HEAD_SIZE ** (-0.5)
    offsets = jnp.arange(tile_length, dtype=jnp.int32)
    query_doc_tiles = block_doc.reshape(tiles_side, tile_length)
    query_span_tiles = block_span.reshape(tiles_side, tile_length)
    numer_list = [
        jnp.zeros((tile_length, pair_heads, query_group_width, HEAD_SIZE), jnp.float32)
        for _ in range(tiles_side)
    ]
    denom_list = [
        jnp.zeros((tile_length, pair_heads, query_group_width), jnp.float32)
        for _ in range(tiles_side)
    ]
    for distance, source, key_doc, key_span in sources:
        key_start = query_start - distance * shard_len
        present = ctx_index >= distance
        key_doc_tiles = key_doc.reshape(tiles_side, tile_length)
        key_span_tiles = key_span.reshape(tiles_side, tile_length)
        live_table = (
            (key_doc_tiles[None, :, tile_length - 1] >= query_doc_tiles[:, None, 0])
            & (key_span_tiles[None, :, tile_length - 1] >= query_span_tiles[:, None, 0])
            & present
        )
        for q_block in range(tiles_side):
            for k_block in range(tiles_side):
                q_first = q_block * tile_length
                k_first = k_block * tile_length
                static_gap = distance * shard_len + q_first - k_first
                if static_gap + tile_length - 1 < 0:
                    continue
                if static_gap - (tile_length - 1) > reach_len - 1:
                    continue

                def compute(
                    inner_acc,
                    source=source,
                    key_start=key_start,
                    q_first=q_first,
                    k_first=k_first,
                    key_doc_tiles=key_doc_tiles,
                    key_span_tiles=key_span_tiles,
                    q_block=q_block,
                    k_block=k_block,
                ):
                    numer_in, denom_in = inner_acc
                    query_tile = grouped[q_first : q_first + tile_length]
                    kv_tile = source[k_first : k_first + tile_length]
                    scores = (
                        jnp.einsum(
                            "qhgd,khd->qhgk",
                            query_tile,
                            kv_tile[:, :, :HEAD_SIZE],
                            preferred_element_type=jnp.float32,
                        )
                        * inv_root
                    )
                    q_pos = query_start + q_first + offsets
                    k_pos = key_start + k_first + offsets
                    q_doc_t = query_doc_tiles[q_block]
                    q_span_t = query_span_tiles[q_block]
                    k_doc_t = key_doc_tiles[k_block]
                    k_span_t = key_span_tiles[k_block]
                    allowed = (
                        (q_doc_t[:, None] == k_doc_t[None, :])
                        & (q_span_t[:, None] == k_span_t[None, :])
                        & (k_pos[None, :] <= q_pos[:, None])
                    )
                    weights = jnp.where(allowed[:, None, None, :], jnp.exp(scores), 0.0)
                    part_den = jnp.sum(weights, axis=3)
                    part_num = jnp.einsum(
                        "qhgk,khd->qhgd",
                        weights.astype(jnp.bfloat16),
                        kv_tile[:, :, HEAD_SIZE:],
                        preferred_element_type=jnp.float32,
                    )
                    return (numer_in + part_num, denom_in + part_den)

                numer_list[q_block], denom_list[q_block] = lax.cond(
                    live_table[q_block, k_block],
                    compute,
                    lambda inner_acc: inner_acc,
                    (numer_list[q_block], denom_list[q_block]),
                )
    numerator = jnp.concatenate(numer_list, axis=0)
    denominator = jnp.concatenate(denom_list, axis=0)
    attended = (
        (numerator / denominator[..., None])
        .astype(jnp.bfloat16)
        .reshape(shard_len, local_heads, HEAD_SIZE)
    )
    returned = lax.all_to_all(attended, "exp", split_axis=0, concat_axis=1, tiled=True)
    return returned.reshape(shard_rows, QUERY_HEADS * HEAD_SIZE)


def routes_of(ctx, z, b, zp, borrowed, blocks, lanes):
    top, even, inner = lanes - 1, ctx % 2 == 0, (z >= 1) & (z < lanes - 1)
    keep = (
        (b == 0) & (zp <= z) & (z < top),
        even & (b <= 1) & (zp >= z) & (z > 0),
        ((b == 0) & (even | ((zp <= z) & (ctx < blocks - 1)))) | ((b == 1) & even & (zp >= z)),
        (b == 0) & even & (ctx < blocks - 2) & (zp >= z),
    )
    lend = (
        ((b == 0) & (zp <= z) & (z < top - 1)) | ((b == 2) & (zp == 0) & (z == 0)),
        (even & (b <= 1) & (zp >= z) & (z >= 2)) | ((ctx % 2 == 1) & (b == 0) & (zp == top) & (z == top)),
        ((b == 0) & ((even & inner) | ((ctx % 2 == 1) & (zp <= z) & (ctx < blocks - 1) & (z >= 1))))
        | ((b == 1) & even & inner & ((zp >= z) | (z == 1))),
        (b == 0) & even & (ctx < blocks - 2) & ((inner & (zp >= z)) | ((z == 0) & (zp == 0))),
    )
    return [(borrowed & l) | ((borrowed ^ True) & k) for k, l in zip(keep, lend)]


def arrives_at(ctx, z, b, zp, borrowed, lanes):
    top, even, inner = lanes - 1, ctx % 2 == 0, (z >= 1) & (z < lanes - 1)
    before, two = (b == 1) & (ctx > 0), (b == 2) & (ctx > 1)
    keep = ((b == 0) & ((zp < z) | ((zp > z) & even))) | before | (two & (zp >= z))
    lend = (
        inner & (
            ((b == 0) & ((zp < z) | ((zp > z) & (even | ((zp == top) & (z == top - 1))))))
            | before | (two & ((zp >= z) | ((z == 1) & (zp == 0))))
        )
    ) | (even & (((z == 0) & two & (zp == 0)) | ((z == top) & before & (zp == top))))
    return (borrowed & lend) | ((borrowed ^ True) & keep)


def seen_from(ctx, z, b, zp):
    return ((b == 0) & (zp <= z)) | ((b == 1) & (ctx > 0)) | ((b == 2) & (ctx > 1) & (zp >= z))


WAIT, WAIT_TAGGED, ATTEND, TAKE, BACK, DONE = range(1, 7)


def plan(blocks, lanes, pairs, lent, knobs, halves=2, fixed=None):
    sequence, backlog, eager, cost = knobs
    hop, wire_time, inside, scalar, block, close = cost
    top = lanes - 1
    devices = [(c, z) for c in range(blocks) for z in range(lanes)]
    clock, events, log = 0, [], {d: [] for d in devices}
    queue, busy, q_parts = {}, {}, {}
    inbox = {d: [] for d in devices}
    got = {d: [] for d in devices}
    issued, at, part_at = dict.fromkeys(devices, 0), dict.fromkeys(devices, 0), dict.fromkeys(devices, 0)
    attended = {d: (set(), set()) for d in devices}
    closed = {d: set() for d in devices}
    idle = dict.fromkeys(devices, True)
    finish_at = dict.fromkeys(devices, 0.0)

    def ward_of(z):
        return 0 if z == 1 else top

    def push(t, kind, what):
        nonlocal clock
        clock += 1
        heapq.heappush(events, (t, clock, kind, what))

    def wire(d, way):
        c, z = d
        if way < 2:
            return ("z", c // 2, z, way)
        return ("in", c, z, 0) if way == 2 and c % 2 == 0 else ("c", c // 2, z, 0)

    def post(t, d, way, message):
        w = wire(d, way)
        queue.setdefault(w, {}).setdefault(d, []).append(message)
        if not busy.get(w):
            busy[w] = True
            push(t, "wire", (w, None))

    def send_slot(t, d, slot, p, parts):
        c, z = d
        b, zp = slot // lanes, slot % lanes
        to = ((c, z + 1, b), (c, z - 1, b), (c + 1, z, b + 1), (c + 2, z, b + 2))
        for way, taken in enumerate(routes_of(c, z, b, zp, p < lent, blocks, lanes)):
            if taken:
                for half in parts:
                    tc, tz, tb = to[way]
                    post(t, d, way, ((tc, tz), (tb * lanes + zp, p, half)))

    def issue(t, d, p):
        c, z = d
        send_slot(t, d, z, p, range(halves))
        if p < lent and z in (0, top):
            for i in range(2 * halves):
                post(t, d, 0 if z == 0 else 1, ((c, 1 if z == 0 else top - 1), (-1, p, i)))

    def give_back(t, d, p):
        for i in range(2 * halves):
            post(t + close, d, 1 if d[1] == 1 else 0, ((d[0], ward_of(d[1])), (-2, p, i)))

    def backlog_of(d, p):
        c, z = d
        used = [w for w, taken in enumerate(routes_of(c, z, 0, z, p < lent, blocks, lanes)) if taken]
        lens = [len(queue.get(wire(d, w), {}).get(d, [])) for w in used if not (w == 2 and c % 2 == 0)]
        if p < lent and z in (0, top):
            lens.append(len(queue.get(wire(d, 0 if z == 0 else 1), {}).get(d, [])))
        return min(lens) if lens else 0

    def wanted(d, target, p):
        c, z = d
        if p >= lent if target else (p < lent and z in (0, top)):
            return []
        return [s for s in range(3 * lanes) if seen_from(c, ward_of(z) if target else z, s // lanes, s % lanes)]

    def replay(t, d):
        c, z = d
        steps = fixed[(z, c % 2)]
        while at[d] < len(steps):
            kind, p, slot, other, target = steps[at[d]]
            b, zp = slot // lanes, slot % lanes
            at[d] += 1
            if kind == WAIT and slot == z:
                issue(t, d, p)
                return scalar
            if kind == WAIT and arrives_at(c, z, b, zp, p < lent, lanes):
                if any(m[1:] == (slot, p, part_at[d]) for m in inbox[d]):
                    send_slot(t + scalar / 2, d, slot, p, (part_at[d],))
                    part_at[d] = (part_at[d] + 1) % halves
                    at[d] -= part_at[d] > 0
                    return scalar
                at[d] -= 1
                return None
            if kind == TAKE and q_parts.get((d, p), 0) < 2 * halves:
                at[d] -= 1
                return None
            if kind == ATTEND and (slot // lanes <= c or other // lanes <= c):
                return scalar + block
            if kind == BACK:
                give_back(t, d, p)
            if kind in (BACK, DONE):
                return close
        return None

    def step(t, d):
        c, z = d
        ahead = eager[0] if z in (0, top) else eager[1]
        order = sequence[0] if z in (0, top) else sequence[1]
        if issued[d] < len(order) and issued[d] < ahead or (
            not inbox[d] and issued[d] < len(order) and backlog_of(d, order[issued[d]]) < backlog
        ):
            p = order[issued[d]]
            issued[d] += 1
            issue(t, d, p)
            got[d].append((z, p))
            log[d].append((WAIT, p, z, z, 0))
            return scalar
        if inbox[d]:
            _, slot, p, half = inbox[d].pop(0)
            send_slot(t + scalar / 2, d, slot, p, (half,))
            if half == halves - 1:
                got[d].append((slot, p))
                log[d].append((WAIT, p, slot, slot, 0))
            return scalar
        for target in (1, 0) if z in (1, top - 1) else (0,):
            for p in range(pairs):
                if target and (q_parts.get((d, p), 0) < 2 * halves or (ward_of(z), 0) not in got[d]):
                    continue
                todo = [s for s in wanted(d, target, p) if (s, p) not in attended[d][target]]
                tag = 0 if p < lent else lent
                ready = [s for s, q in got[d] if q == p and s in todo and (s, tag) in got[d]]
                if len(ready) > 1 or len(ready) == len(todo) == 1:
                    if target and ("q", p) not in closed[d]:
                        closed[d].add(("q", p))
                        log[d].append((TAKE, p, 0, 0, 1))
                    attended[d][target].update((s, p) for s in ready[:2])
                    log[d].append((ATTEND, p, ready[0], ready[min(1, len(ready) - 1)], target))
                    return scalar + block
                if not todo and wanted(d, target, p) and (target, p) not in closed[d]:
                    closed[d].add((target, p))
                    log[d].append((BACK if target else DONE, p, 0, 0, target))
                    if target:
                        give_back(t, d, p)
                    return close
        return None

    for d in devices:
        push(0.0, "go", d)
    while events:
        t, _, kind, what = heapq.heappop(events)
        if kind == "wire":
            w, last = what
            lines = [(d, q) for d, q in sorted(queue[w].items()) if q]
            if not lines:
                busy[w] = False
                continue
            d, q = ([x for x in lines if x[0] != last] or lines)[0]
            to, message = q.pop(0)
            length = inside if w[0] == "in" else wire_time
            push(t + length, "wire", (w, d))
            push(t + length + hop, "come", (to, message))
            wake = d
        elif kind == "come":
            wake, message = what
            finish_at[wake] = max(finish_at[wake], t)
            if message[0] >= 0:
                inbox[wake].append((t,) + message)
            elif message[0] == -1:
                q_parts[(wake, message[1])] = q_parts.get((wake, message[1]), 0) + 1
        else:
            length = (replay if fixed else step)(t, what)
            idle[what] = length is None
            if length is not None:
                finish_at[what] = max(finish_at[what], t + length)
                push(t + length, "go", what)
            continue
        if idle[wake]:
            idle[wake] = False
            push(t, "go", wake)
    if fixed:
        assert all(at[c, z] == len(fixed[z, c % 2]) for c, z in devices)
    return log, finish_at


def roles_of(log, blocks, lanes):
    middle = 2 * (blocks // 4)
    return {(z, parity): log[middle + parity, z] for z in range(lanes) for parity in range(2)}


HALVES = 2
TAG_ROWS = 16
LENT_PAIRS = 1
KNOBS = (([1, 2, 0, 3], [1, 0, 3, 2]), 1, (2, 4), (1.8, 1.43, 0.18, 0.08, 0.55, 0.4))
FAR = 1 << 20

PAIR_AT, SLOT_AT, OTHER_AT, FLAG_AT = 3, 6, 11, 16
OWN, QUERIES, FOR_WARD, ALONE = (1 << (FLAG_AT + i) for i in range(4))
WAY_AT = FLAG_AT + 4
SLOT_1, SLOT_2, OTHER_1, OTHER_2 = (1 << (WAY_AT + 4 + i) for i in range(4))


def unit_tile(tile):
    widened = tile.astype(jnp.float32)
    factor = lax.rsqrt(jnp.mean(widened * widened, axis=-1, keepdims=True) + 1e-06)
    return (widened * factor).astype(jnp.bfloat16)


def coded_steps(blocks, lanes, pairs, lent):
    roles = roles_of(plan(blocks, lanes, pairs, lent, KNOBS, 1)[0], blocks, lanes)
    coded = {}
    for (z, parity), steps in roles.items():
        ctx = 2 * (blocks // 4) + parity
        coded[z, parity] = []
        for kind, p, slot, other, target in steps:
            b, b2 = slot // lanes, other // lanes
            if kind == WAIT and p in (0, lent):
                kind = WAIT_TAGGED
            value = kind | p << PAIR_AT | slot << SLOT_AT | other << OTHER_AT | FOR_WARD * target
            value |= SLOT_1 * (b == 1) | SLOT_2 * (b == 2) | OTHER_1 * (b2 == 1) | OTHER_2 * (b2 == 2)
            if kind <= WAIT_TAGGED:
                ways = routes_of(ctx, z, b, slot % lanes, p < lent, blocks, lanes)
                value |= sum(int(taken) << (WAY_AT + way) for way, taken in enumerate(ways))
                value |= OWN * (slot == z)
                value |= QUERIES * (slot == z and p < lent and z in (0, lanes - 1))
            else:
                value |= ALONE * (slot == other)
            coded[z, parity].append(value)
    return coded


def sent_counts(blocks, lanes, pairs, lent):
    sent = [[[0] * (blocks * lanes) for _ in range(2)] for _ in range(4)]
    for ctx in range(blocks):
        for z in range(lanes):
            for slot in range(3 * lanes):
                for p in range(pairs):
                    b, zp = slot // lanes, slot % lanes
                    if slot == z or arrives_at(ctx, z, b, zp, p < lent, lanes):
                        for way, taken in enumerate(routes_of(ctx, z, b, zp, p < lent, blocks, lanes)):
                            sent[way][p in (0, lent)][ctx * lanes + z] += taken
    return sent


def relay_kernel(
    blocks, lanes, pairs, lent, steps, q_ref, k_ref, v_ref, doc_ref, span_ref, out_ref,
    q_raw, k_raw, v_raw, id_raw, q_unit, kv, col, acc, back, table,
    own_sem, recv_sem, send_sem, q_send, q_recv, back_send, back_recv,
):
    rows = k_ref.shape[0]
    top = lanes - 1
    ctx = lax.axis_index("ctx")
    z = lax.axis_index("exp")
    even = ctx % 2 == 0
    helper = (z == 1) | (z == top - 1)
    is_end = (z == 0) | (z == top)
    ward = jnp.where(z == 1, 0, top)
    mate = jnp.where(z == 0, 1, jnp.where(z == top, top - 1, ward))
    half_rows = 2 * rows
    pair_rows = HALVES * half_rows
    piece = pair_rows + TAG_ROWS
    length = max(len(s) for s in steps.values())
    sent = sent_counts(blocks, lanes, pairs, lent)

    barrier = pltpu.get_barrier_semaphore()
    neighbours = [
        (z > 0, (ctx, z - 1)), (z < top, (ctx, z + 1)),
        (ctx > 0, (ctx - 1, z)), (ctx < blocks - 1, (ctx + 1, z)),
        (even & (ctx > 1), (ctx - 2, z)), (even & (ctx < blocks - 2), (ctx + 2, z)),
    ]
    for present, device in neighbours:
        @pl.when(present)
        def _(device=device):
            pl.semaphore_signal(barrier, inc=1, device_id=device, device_id_type=MESH)

    loads = [
        pltpu.make_async_copy(ref, dst, own_sem.at[i])
        for i, (ref, dst) in enumerate(
            [(k_ref, k_raw), (v_ref, v_raw), (doc_ref, id_raw.at[pl.ds(0, 1)]), (span_ref, id_raw.at[pl.ds(1, 1)]), (q_ref, q_raw)]
        )
    ]
    for load in loads:
        load.start()

    role = z * 2 + ctx % 2
    lost_1 = jnp.where(ctx < 1, SLOT_1, 0) | jnp.where(ctx < 2, SLOT_2, 0)
    lost_2 = jnp.where(ctx < 1, OTHER_1, 0) | jnp.where(ctx < 2, OTHER_2, 0)
    shut = jnp.where(ctx == blocks - 1, 1 << (WAY_AT + 2), 0) | jnp.where(ctx >= blocks - 2, 1 << (WAY_AT + 3), 0)
    listed = {}
    own_length = jnp.int32(0)
    for (zz, parity), codes in steps.items():
        own_length = jnp.where(role == zz * 2 + parity, len(codes), own_length)
    for k in range(length):
        value = jnp.int32(0)
        for (zz, parity), codes in steps.items():
            if k < len(codes):
                value = jnp.where(role == zz * 2 + parity, codes[k], value)
        first_lost, second_lost = (value & lost_1) != 0, (value & lost_2) != 0
        waits = (value & 7) <= WAIT_TAGGED
        other = jnp.where(second_lost, value >> SLOT_AT, value >> OTHER_AT) & 31
        slot = jnp.where(first_lost, value >> OTHER_AT, value >> SLOT_AT) & 31
        fixed = (value & ~(1023 << SLOT_AT)) | slot << SLOT_AT | other << OTHER_AT
        fixed = fixed | jnp.where(first_lost | second_lost, ALONE, 0)
        fixed = jnp.where(first_lost & second_lost, 0, fixed)
        final = jnp.where(waits, jnp.where(first_lost, 0, value & ~shut), fixed)
        table[k] = final
        if any(k < len(codes) and codes[k] & 7 == ATTEND for codes in steps.values()):
            listed[k] = final

    place = ctx * lanes + z
    holds = [[jnp.int32(0)] * 2 for _ in range(4)]
    for way in range(4):
        for tag in range(2):
            for i, number in enumerate(sent[way][tag]):
                holds[way][tag] = jnp.where(place == i, number, holds[way][tag])
    acc[...] = jnp.zeros_like(acc)
    for load in loads[:4]:
        load.wait()
    docs = jnp.broadcast_to(id_raw[0:1, :].astype(jnp.float32), (TAG_ROWS, rows))
    spans = jnp.broadcast_to(id_raw[1:2, :].astype(jnp.float32), (TAG_ROWS, rows))
    first = lax.broadcasted_iota(jnp.int32, (TAG_ROWS, rows), 0) == 0
    tags = jnp.where(first, docs, spans).astype(jnp.bfloat16)
    for p in range(pairs):
        for half in range(HALVES):
            column = (p * HALVES + half) * HEAD_SIZE
            kv[z * pairs + p, half * half_rows : half * half_rows + rows, :] = unit_tile(k_raw[:, column : column + HEAD_SIZE])
            kv[z * pairs + p, half * half_rows + rows : (half + 1) * half_rows, :] = v_raw[:, column : column + HEAD_SIZE]
        if p in (0, lent):
            kv[z * pairs + p, pair_rows : pair_rows + TAG_ROWS, :] = tags

    def code_of(slot, p):
        ids = kv[slot * pairs + p, pair_rows : pair_rows + TAG_ROWS, :].astype(jnp.float32)
        return jnp.broadcast_to(ids[0:1, :] * 256.0 + ids[1:2, :], (rows, rows))

    loads[4].wait()
    for p in range(pairs):
        for half in range(HALVES):
            for j in range(GROUP):
                column = ((p * HALVES + half) * GROUP + j) * HEAD_SIZE
                q_unit[p, half, j * rows : (j + 1) * rows, :] = unit_tile(q_raw[:, column : column + HEAD_SIZE])
    col[0] = code_of(z, 0).T

    pl.semaphore_wait(barrier, sum(present.astype(jnp.int32) for present, _ in neighbours))

    def copy(way, slot, p, size, device, to_slot):
        return pltpu.make_async_remote_copy(
            src_ref=kv.at[slot * pairs + p, pl.ds(0, size)],
            dst_ref=kv.at[to_slot * pairs + p, pl.ds(0, size)],
            send_sem=send_sem.at[way, int(size > pair_rows)],
            recv_sem=recv_sem.at[to_slot, p],
            device_id=device,
            device_id_type=MESH,
        )

    def query_copy(p):
        return pltpu.make_async_remote_copy(
            src_ref=q_unit.at[p], dst_ref=q_unit.at[pairs + p], send_sem=q_send.at[p], recv_sem=q_recv.at[p],
            device_id=(ctx, mate), device_id_type=MESH,
        )

    def back_copy(p, half):
        columns = pl.ds((p * HALVES + half) * GROUP * HEAD_SIZE, GROUP * HEAD_SIZE)
        return pltpu.make_async_remote_copy(
            src_ref=back.at[:, columns], dst_ref=out_ref.at[:, columns],
            send_sem=back_send.at[p, half], recv_sem=back_recv.at[p, half],
            device_id=(ctx, mate), device_id_type=MESH,
        )

    scale = math.log2(math.e) * HEAD_SIZE ** (-0.5)

    def attend(step):
        p = (step >> PAIR_AT) & 7
        slots = [(step >> SLOT_AT) & 31, (step >> OTHER_AT) & 31]
        for_ward = (step & FOR_WARD) != 0
        which = jnp.where(for_ward, 1, 0)
        lane = jnp.where(for_ward, ward, z)
        at = jnp.where(for_ward, pairs + p, p)
        tag = jnp.where(p < lent, 0, lent)
        ahead = lax.broadcasted_iota(jnp.int32, (rows, rows), 1) - lax.broadcasted_iota(jnp.int32, (rows, rows), 0)
        kept = []
        for i, slot in enumerate(slots):
            gap = (2 * lanes * lax.div(slot, lanes) + lane - slot) * rows
            if i == 1:
                gap = jnp.where((step & ALONE) != 0, -FAR, gap)
            near = jnp.where(col[which] == code_of(slot, tag), ahead, FAR) <= gap
            kept.append(near.astype(jnp.float32).astype(jnp.bfloat16))
        kept = jnp.concatenate(kept, axis=1)
        ones = jnp.ones((2 * rows, HEAD_SIZE), jnp.bfloat16)
        for half in range(HALVES):
            start = half * half_rows
            keys = jnp.concatenate([kv[slot * pairs + p, start : start + rows, :] for slot in slots], axis=0)
            scores = lax.dot_general(
                q_unit[at, half], keys, (((1,), (1,)), ((), ())), preferred_element_type=jnp.float32
            )
            weights = jnp.exp2(scores * scale).astype(jnp.bfloat16)
            weights = jnp.concatenate([weights[j * rows : (j + 1) * rows] * kept for j in range(GROUP)], axis=0)
            values = jnp.concatenate([kv[slot * pairs + p, start + rows : start + half_rows, :] for slot in slots], axis=0)
            acc[at, half] += jnp.dot(
                weights, jnp.concatenate([values, ones], axis=1), preferred_element_type=jnp.float32
            )

    def finish(at, p, to, halves=range(HALVES)):
        for half in halves:
            for j in range(GROUP):
                column = pl.multiple_of(((p * HALVES + half) * GROUP + j) * HEAD_SIZE, HEAD_SIZE)
                part = acc[at, half, j * rows : (j + 1) * rows, :]
                to[:, pl.ds(column, HEAD_SIZE)] = (part[:, :HEAD_SIZE] / part[:, HEAD_SIZE:]).astype(jnp.bfloat16)

    @pl.loop(0, own_length)
    def _(k):
        step = table[k]
        kind = step & 7
        p = (step >> PAIR_AT) & 7
        slot = (step >> SLOT_AT) & 31

        def pass_on(size):
            here = (step & OWN) != 0

            @pl.when(~here)
            def _():
                copy(0, slot, p, size, (ctx, z), slot).wait_recv()

            for way, device, shift in ((0, (ctx, z + 1), 0), (1, (ctx, z - 1), 0), (3, (ctx + 2, z), 2), (2, (ctx + 1, z), 1)):
                @pl.when((step & (1 << (WAY_AT + way))) != 0)
                def _(way=way, device=device, shift=shift):
                    copy(way, slot, p, size, device, slot + shift * lanes).start()

            @pl.when((step & QUERIES) != 0)
            def _():
                query_copy(p).start()

        @pl.when(kind <= WAIT_TAGGED)
        def _():
            @pl.when(kind == WAIT)
            def _():
                pass_on(pair_rows)

            @pl.when(kind == WAIT_TAGGED)
            def _():
                pass_on(piece)

        @pl.when(kind == ATTEND)
        def _():
            chosen = jnp.int32(0)
            for i, value in listed.items():
                chosen = jnp.where(k == i, value, chosen)
            attend(chosen)

        @pl.when(kind > ATTEND)
        def _():
            for own_p in range(pairs):
                @pl.when((kind == DONE) & (p == own_p))
                def _(own_p=own_p):
                    finish(own_p, own_p, out_ref)

            for own_p in range(lent):
                @pl.when((kind == TAKE) & (p == own_p))
                def _(own_p=own_p):
                    query_copy(own_p).wait_recv()
                    if own_p == 0:
                        col[1] = code_of(ward, 0).T

                @pl.when((kind == BACK) & (p == own_p))
                def _(own_p=own_p):
                    for half in range(HALVES):
                        finish(pairs + own_p, own_p, back, (half,))
                        back_copy(own_p, half).start()

    for way in range(4):
        for tag in range(2):
            size = pair_rows + TAG_ROWS * tag
            for number in sorted(set(sent[way][tag]) - {0}):
                @pl.when(holds[way][tag] == number)
                def _(way=way, tag=tag, size=size, number=number):
                    whole = kv.at[pl.ds(0, number), pl.ds(0, size)]
                    pltpu.make_async_remote_copy(
                        src_ref=whole, dst_ref=whole, send_sem=send_sem.at[way, tag], recv_sem=recv_sem.at[0, 0],
                        device_id=(ctx, z), device_id_type=MESH,
                    ).wait_send()

    for p in range(lent):
        @pl.when(is_end)
        def _(p=p):
            query_copy(p).wait_send()
            for half in range(HALVES):
                back_copy(p, half).wait_recv()

        @pl.when(helper)
        def _(p=p):
            for half in range(HALVES):
                back_copy(p, half).wait_send()


def relayed(queries, keys, values, doc_ids, span_ids):
    lanes = lax.axis_size("exp")
    blocks = lax.axis_size("ctx")
    rows = queries.shape[0]
    count = 3 * lanes
    pairs = KEY_VALUE_HEADS // HALVES
    lent = LENT_PAIRS
    steps = coded_steps(blocks, lanes, pairs, lent)
    length = max(len(s) for s in steps.values())
    bf16, f32 = jnp.bfloat16, jnp.float32
    stack = GROUP * rows
    return pl.pallas_call(
        lambda *refs: relay_kernel(blocks, lanes, pairs, lent, steps, *refs),
        out_shape=pltpu.VMEM(queries.shape, bf16),
        in_specs=[pl.BlockSpec(memory_space=pltpu.HBM)] * 5,
        out_specs=pl.BlockSpec(memory_space=pltpu.VMEM),
        scratch_shapes=[
            pltpu.VMEM(queries.shape, bf16),
            pltpu.VMEM(keys.shape, bf16),
            pltpu.VMEM(values.shape, bf16),
            pltpu.VMEM((2, rows), jnp.int32),
            pltpu.VMEM((pairs + lent, HALVES, stack, HEAD_SIZE), bf16),
            pltpu.VMEM((count * pairs, HALVES * 2 * rows + TAG_ROWS, HEAD_SIZE), bf16),
            pltpu.VMEM((2, rows, rows), f32),
            pltpu.VMEM((pairs + lent, HALVES, stack, 2 * HEAD_SIZE), f32),
            pltpu.VMEM((rows, lent * HALVES * GROUP * HEAD_SIZE), bf16),
            pltpu.SMEM((length,), jnp.int32),
            pltpu.SemaphoreType.DMA((5,)),
            pltpu.SemaphoreType.DMA((count, pairs)),
            pltpu.SemaphoreType.DMA((4, 2)),
            pltpu.SemaphoreType.DMA((lent,)),
            pltpu.SemaphoreType.DMA((lent,)),
            pltpu.SemaphoreType.DMA((lent, HALVES)),
            pltpu.SemaphoreType.DMA((lent, HALVES)),
        ],
        compiler_params=pltpu.CompilerParams(collective_id=0, has_side_effects=True, vmem_limit_bytes=60 << 20),
    )(queries, keys, values, doc_ids[None, :], span_ids[None, :])


def per_device(queries, keys, values, doc_ids, span_ids):
    lanes, blocks = lax.axis_size("exp"), lax.axis_size("ctx")
    rows = queries.shape[0]
    tokens = rows * lanes * blocks
    reach = min(SPAN, DOC_LEN if tokens > PACKED_TOKENS else DOC_TOP)
    if reach <= 2 * lanes * rows and blocks % 2 == 0 and blocks >= 6 and 4 <= lanes <= 8 and rows == HEAD_SIZE:
        return relayed(queries, keys, values, doc_ids, span_ids)
    return general(queries, keys, values, doc_ids, span_ids)


def solution(mesh):
    in_specs = (
        P(("ctx", "exp"), None),
        P(("ctx", "exp"), None),
        P(("ctx", "exp"), None),
        P(("ctx", "exp")),
        P(("ctx", "exp")),
    )
    out_specs = P(("ctx", "exp"), None)
    return jax.shard_map(
        per_device, mesh=mesh, in_specs=in_specs, out_specs=out_specs, check_vma=False
    )
```
